32 devices in a mesh: grp: 2 (over x), seq: 4 (over y, core), sub: 4 (over z).
Axes of the slice: x: 2, y: 2, z: 4, core: 2. Of those that a mesh axis runs over, the one named last changes fastest.
Arguments:
- query_rows: bfloat16 [8, 512, 2048], P(('grp', 'sub'), 'seq'), parts along dimension 0, may hold values from -9 to 9
- key_rows: bfloat16 [8, 512, 256], P(('grp', 'sub'), 'seq'), parts along dimension 0, may hold values from -4 to 4
- value_rows: bfloat16 [8, 512, 256], P(('grp', 'sub'), 'seq'), parts along dimension 0, may hold values from -6 to 6
- residual_in: bfloat16 [8, 512, 2048], P(('grp', 'sub'), 'seq'), parts along dimension 0, may hold values from -6 to 6
- out_proj: bfloat16 [2048, 2048], P('seq'), may hold values from -0.5 to 0.5
- norm_gain: bfloat16 [2048], replicated, may hold values from 0.099609375 to 1.8984375
- expert_ids: int32 [8, 512, 8], P(('grp', 'sub'), 'seq'), parts along dimension 0, may hold values from 0 to 15, all different within a row; in each aligned block of 128 rows (0 to 127, 128 to 255, ..., all dimensions but the last counted through in order) at most 80 rows name the same one
- gate_weights: bfloat16 [8, 512, 8], P(('grp', 'sub'), 'seq'), parts along dimension 0, may hold values from 0.049804688 to 1
- expert_gate: bfloat16 [16, 2048, 768], P(('seq', 'sub')), may hold values from -0.125 to 0.125
- expert_up: bfloat16 [16, 2048, 768], P(('seq', 'sub')), may hold values from -0.125 to 0.125
- expert_down: bfloat16 [16, 768, 2048], P(('seq', 'sub')), may hold values from -0.21875 to 0.21875
Outputs:
- layer_out: bfloat16 [8, 512, 2048], P(('grp', 'sub'), 'seq'), parts along dimension 0
The draws below stay inside these ranges and needn't reach their ends.
There are 2 independent parts, one for each index of `grp`. The reference program is written for one: setup_inputs(seed, part) draws one part's arguments, and reference() takes and returns one part's arrays. A program takes and returns all parts, laid end to end along the dimension named above; an argument that names none is the same for every part. Nothing has to cross between parts.
Inputs may be any that keep to these rules, and one draw needn't show every extreme that they name: `expert_ids`: A row names 8 different experts. In each aligned block of 128 rows (the rows of one device) no expert is named by more than 80 rows, a bound that some block reaches.
All inputs are finite; a program needn't handle non-finite values.
Results may differ from the reference program's by a relative error of at most 0.013.
Values may be sent and summed in bfloat16 or wider, within the bound.
A program may use at most 128 MiB of HBM per device.

```python
import math
import jax
import jax.numpy as jnp
import numpy as np
from jax import lax

D = 2048
HD = 128
QH = 16
KVH = 2
FF = 768
TOPK = 8
TOK_DEV = 128
SEQS = 4
SEQ_LEN = 512
EXPERTS = 16
CAP = 80


def draw_attention(key):
    query_key = jax.random.fold_in(key, 101)
    other_key = jax.random.fold_in(key, 202)
    query_shape = (SEQS, SEQ_LEN, QH * HD)
    key_shape = (SEQS, SEQ_LEN, KVH * HD)
    queries = 2.0 * jax.random.truncated_normal(query_key, -4.0, 4.0, query_shape, jnp.float32)
    keys = jax.random.truncated_normal(other_key, -4.0, 4.0, key_shape, jnp.float32)
    return (queries, keys)


def draw_query_rows(key, part):
    return draw_attention(key)[0].astype(jnp.bfloat16)


def draw_key_rows(key, part):
    return draw_attention(key)[1].astype(jnp.bfloat16)


def steps_of(rng, shape, split, least, largest):
    loudness, own = 1.0, jax.random.fold_in(rng, 6)
    for axis_at, parts in split:
        heights = jnp.exp(jax.random.uniform(jax.random.fold_in(own, axis_at), (parts,), jnp.float32, least / len(split), largest / len(split)))
        loudness = loudness * jnp.repeat(heights, shape[axis_at] // parts).reshape([-1 if axis == axis_at else 1 for axis in range(len(shape))])
    return loudness


def assign_block(key, own, number, rows, number_of, top, bound, skew):
    order = jax.random.permutation(key, number_of)
    crowded, common = load_shares(number_of, rows * top, bound, skew, True), load_shares(number_of, rows * top, bound, skew, False)
    places = jnp.arange(number_of)

    def named(tallies, turn):
        used = int((tallies > 0).sum())
        fixed = max(1, used // 4)
        moved = fixed + (places - fixed + turn * (used - fixed)) % max(1, number_of - fixed)
        return jnp.zeros((number_of,), jnp.int32).at[order[jnp.where(places < fixed, places, moved)]].set(jnp.asarray(tallies, jnp.int32))

    tallies = jnp.where(number % 4 == 0, named(crowded, number // 4), named(common, number - number // 4 - 1))
    mixed = jax.random.permutation(jax.random.fold_in(own, 3), number_of)
    giver, taker = mixed[0:number_of // 2 * 2:2], mixed[1:number_of // 2 * 2:2]
    slack = jnp.minimum(tallies[giver] - 1, bound - tallies[taker]) // 2
    slack = jnp.where((giver == order[0]) | (taker == order[0]) | (tallies[taker] == 0), 0, jnp.maximum(slack, 0))
    moved = jax.random.randint(jax.random.fold_in(own, 4), (number_of // 2,), 0, 1 << 20) % (slack + 1)
    tallies = tallies.at[giver].add(-moved).at[taker].add(moved)
    members = jnp.searchsorted(jnp.cumsum(tallies), jnp.arange(rows * top), side="right").astype(jnp.int32)
    listing = members.reshape(top, rows).T
    listing = listing[jax.random.permutation(jax.random.fold_in(own, 1), rows)]
    turn = jax.random.randint(jax.random.fold_in(own, 2), (rows, 1), 0, top)
    return jnp.take_along_axis(listing, (jnp.arange(top)[None, :] + turn) % top, axis=1)


def load_shares(count, total, bound, slope, full):
    weights = [(1 << 20) // math.isqrt(grade ** slope) + 1 for grade in range(1, count + 1)]
    largest = bound if full else min(bound, max(-(-total // count), total * weights[0] // sum(weights)))
    least = 1 if total - largest >= count - 1 else 0
    given, rest = [largest] + [least] * (count - 1), total - largest - least * (count - 1)
    while rest > 0:
        movable = [i for i in range(1, count) if given[i] < largest] or [i for i in range(1, count) if given[i] < bound]
        whole, left = sum([weights[i] for i in movable]), rest
        for i in movable:
            addition = min(bound - given[i], max(1, left * weights[i] // whole), rest)
            given[i] = given[i] + addition
            rest = rest - addition
    return np.array(given)


def centred(stream_key, shape, deviation, limit, cuts=(), held_as=jnp.bfloat16):
    values = deviation * jax.random.normal(stream_key, shape, jnp.float32)
    if cuts:
        values = values * steps_of(stream_key, shape, cuts, -0.22, 0.18)
    return jnp.clip(values, -limit, limit).astype(held_as)


def setup_inputs(seed: int = 0, part: int = 0) -> dict:
    seeds = jax.random.split(jax.random.key(seed), 12)
    part_keys = jax.random.split(jax.random.fold_in(seeds[11], part), 12)
    query_rows = draw_query_rows(jax.random.fold_in(jax.random.fold_in(seeds[11], part), 71), part)
    key_rows = draw_key_rows(jax.random.fold_in(jax.random.fold_in(seeds[11], part), 71), part)
    value_rows = centred(part_keys[2], (SEQS, SEQ_LEN, KVH * HD), 1.0, 6.0, ((0, 4), (1, 4)))
    residual_in = centred(part_keys[3], (SEQS, SEQ_LEN, D), 1.0, 6.0, ((0, 4), (1, 4)))
    out_proj = centred(seeds[4], (QH * HD, D), HD ** -0.5, 0.5, ((0, 4),))
    norm_gain = jnp.clip(1.0 + 0.18 * jax.random.normal(seeds[5], (D,), jnp.float32), 0.099609375, 1.8984375).astype(jnp.bfloat16)
    expert_ids_keys = jax.random.split(jax.random.fold_in(part_keys[6], 1), SEQS * SEQ_LEN // TOK_DEV)
    expert_ids_turns = jax.random.permutation(jax.random.fold_in(part_keys[6], 3), SEQS * SEQ_LEN // TOK_DEV)
    expert_ids = jax.vmap(lambda own, number: assign_block(jax.random.fold_in(part_keys[6], 2), own, number, TOK_DEV, EXPERTS, TOPK, CAP, 2))(expert_ids_keys, expert_ids_turns).reshape((SEQS, SEQ_LEN, TOPK))
    gate_weights = jnp.clip(jnp.exp(math.log(1.0) - 2.9996462 * jax.random.uniform(part_keys[7], (SEQS, SEQ_LEN, TOPK), jnp.float32) ** steps_of(part_keys[7], (SEQS, SEQ_LEN, TOPK), ((0, 4), (1, 4)), -0.2, 0.2)), 0.049804688, 1.0).astype(jnp.bfloat16)
    expert_gate = centred(seeds[8], (EXPERTS, D, FF), D ** -0.5, 0.125, ((0, 16),))
    expert_up = centred(seeds[9], (EXPERTS, D, FF), D ** -0.5, 0.125, ((0, 16),))
    expert_down = centred(seeds[10], (EXPERTS, FF, D), FF ** -0.5, 0.21875, ((0, 16),))
    return {"query_rows": query_rows, "key_rows": key_rows, "value_rows": value_rows, "residual_in": residual_in, "out_proj": out_proj, "norm_gain": norm_gain, "expert_ids": expert_ids, "gate_weights": gate_weights, "expert_gate": expert_gate, "expert_up": expert_up, "expert_down": expert_down}


def reference(query_rows, key_rows, value_rows, residual_in, out_proj, norm_gain, expert_ids, gate_weights, expert_gate, expert_up, expert_down):
    group = QH // KVH
    scale = 1.0 / HD ** 0.5
    length = SEQ_LEN
    query_heads = query_rows.reshape(SEQS, length, QH, HD).transpose(0, 2, 1, 3).reshape(SEQS * QH, length, HD)
    key_heads = key_rows.reshape(SEQS, length, KVH, HD).transpose(0, 2, 1, 3)
    value_heads = value_rows.reshape(SEQS, length, KVH, HD).transpose(0, 2, 1, 3)
    positions = jnp.arange(length, dtype=jnp.int32)
    causal = positions[:, None] >= positions[None, :]

    def one_head(index):
        seq_index = index // QH
        kv_index = index % QH // group
        scores = jnp.dot(query_heads[index].astype(jnp.float32), key_heads[seq_index, kv_index].astype(jnp.float32).T, precision=lax.Precision.HIGHEST) * scale
        scores = jnp.where(causal, scores, -1e+30)
        peak = lax.optimization_barrier(jnp.max(scores, axis=1, keepdims=True))
        weights = jnp.exp(scores - peak)
        probs = (weights / lax.optimization_barrier(jnp.sum(weights, axis=1, keepdims=True))).astype(jnp.bfloat16)
        probs = lax.optimization_barrier(probs)
        return jnp.dot(probs.astype(jnp.float32), value_heads[seq_index, kv_index].astype(jnp.float32), precision=lax.Precision.HIGHEST).astype(jnp.bfloat16)
    head_out = lax.map(one_head, jnp.arange(SEQS * QH, dtype=jnp.int32))
    attended = head_out.reshape(SEQS, QH, length, HD).transpose(0, 2, 1, 3).reshape(SEQS * length, QH * HD)
    projected = jnp.dot(attended, out_proj, preferred_element_type=jnp.float32)
    hidden = (residual_in.reshape(SEQS * length, D).astype(jnp.float32) + projected).astype(jnp.bfloat16)
    wide = hidden.astype(jnp.float32)
    normed = (wide * lax.rsqrt(lax.optimization_barrier(jnp.mean(wide * wide, axis=1, keepdims=True)) + 1e-06) * norm_gain.astype(jnp.float32)).astype(jnp.bfloat16)
    rows = SEQS * length
    flat_ids = expert_ids.reshape(-1).astype(jnp.int32)
    assigned = flat_ids.shape[0]
    flat_gates = gate_weights.reshape(-1)
    order = jnp.argsort(flat_ids, stable=True).astype(jnp.int32)
    sorted_ids = flat_ids[order]
    counts = jnp.zeros((EXPERTS,), jnp.int32).at[flat_ids].add(1)
    tiles = (counts + 127) // 128
    tile_end = jnp.cumsum(tiles).astype(jnp.int32)
    tile_first = tile_end - tiles
    row_first = (jnp.cumsum(counts) - counts).astype(jnp.int32)
    position = tile_first[sorted_ids] * 128 + jnp.arange(assigned, dtype=jnp.int32) - row_first[sorted_ids]
    n_tiles = assigned // 128 + EXPERTS
    slot_item = jnp.full((n_tiles * 128,), assigned, jnp.int32).at[position].set(order)
    tile_index = jnp.arange(n_tiles, dtype=jnp.int32)
    tile_owner = jnp.minimum(lax.optimization_barrier(jnp.sum((tile_end[None, :] <= tile_index[:, None]).astype(jnp.int32), axis=1)), EXPERTS - 1)
    padded_rows = jnp.concatenate([normed, jnp.zeros((1, D), jnp.bfloat16)], axis=0)
    padded_gates = jnp.concatenate([flat_gates, jnp.zeros((1,), jnp.bfloat16)], axis=0)
    slot_token = jnp.where(slot_item < assigned, slot_item // TOPK, rows).astype(jnp.int32)

    def tile_step(total, tile):
        owner = tile_owner[tile]
        tokens_here = lax.dynamic_slice_in_dim(slot_token, tile * 128, 128)
        items = lax.dynamic_slice_in_dim(slot_item, tile * 128, 128)
        inputs = padded_rows[tokens_here].astype(jnp.float32)
        gate_proj = jnp.dot(inputs, expert_gate[owner].astype(jnp.float32), precision=lax.Precision.HIGHEST)
        up_proj = jnp.dot(inputs, expert_up[owner].astype(jnp.float32), precision=lax.Precision.HIGHEST)
        inner = lax.optimization_barrier((jax.nn.silu(gate_proj) * up_proj).astype(jnp.bfloat16))
        result = jnp.dot(inner.astype(jnp.float32), expert_down[owner].astype(jnp.float32), precision=lax.Precision.HIGHEST)
        result = result * padded_gates[items].astype(jnp.float32)[:, None]
        rounded = lax.optimization_barrier(result.astype(jnp.bfloat16))
        return (total.at[tokens_here].add(rounded.astype(jnp.float32)), None)
    total, _ = lax.scan(tile_step, jnp.zeros((rows + 1, D), jnp.float32), tile_index)
    layer_out = (wide + total[:rows]).astype(jnp.bfloat16)
    return layer_out.reshape(SEQS, length, D)
```

```python
import functools
import jax
import jax.numpy as jnp
from jax import lax
from jax.experimental import pallas as pl
from jax.experimental.pallas import tpu as pltpu
from jax.sharding import PartitionSpec as P

D = 2048
HD = 128
QH = 16
KVH = 2


def attend_head(queries, keys_one, values_one, block):
    length = queries.shape[0]
    scale = 1.0 / queries.shape[1] ** 0.5
    pieces = []
    for part_index in range(length // block):
        stop = (part_index + 1) * block
        rows_here = queries[part_index * block : stop]
        scores = (
            jnp.einsum("qd,kd->qk", rows_here, keys_one[:stop], preferred_element_type=jnp.float32)
            * scale
        )
        row_pos = part_index * block + jnp.arange(block, dtype=jnp.int32)
        col_pos = jnp.arange(stop, dtype=jnp.int32)
        scores = jnp.where(row_pos[:, None] >= col_pos[None, :], scores, -1e30)
        peak = jnp.max(scores, axis=1, keepdims=True)
        weights = jnp.exp(scores - peak)
        probs = (weights / jnp.sum(weights, axis=1, keepdims=True)).astype(jnp.bfloat16)
        pieces.append(
            jnp.dot(probs, values_one[:stop], preferred_element_type=jnp.float32).astype(
                jnp.bfloat16
            )
        )
    return jnp.concatenate(pieces, axis=0)


def rank_in_expert(flat_ids, experts):
    items = flat_ids.shape[0]
    width = 128
    n_parts = items // width
    onehot = (
        (flat_ids[:, None] == jnp.arange(experts, dtype=jnp.int32)[None, :])
        .astype(jnp.bfloat16)
        .reshape(n_parts, width, experts)
    )
    lower = (
        jnp.arange(width, dtype=jnp.int32)[:, None] > jnp.arange(width, dtype=jnp.int32)[None, :]
    ).astype(jnp.bfloat16)
    within = jnp.einsum("ij,bje->bie", lower, onehot, preferred_element_type=jnp.float32)
    part_counts = jnp.sum(onehot.astype(jnp.float32), axis=1)
    earlier = jnp.cumsum(part_counts, axis=0) - part_counts
    ranks = jnp.sum((within + earlier[:, None, :]) * onehot.astype(jnp.float32), axis=2)
    return ranks.reshape(items).astype(jnp.int32)


def per_device_routed(
    query_rows,
    key_rows,
    value_rows,
    residual_in,
    out_proj,
    norm_gain,
    expert_ids,
    gate_weights,
    expert_gate,
    expert_up,
    expert_down,
):
    tokens = query_rows.shape[1]
    n_seq = lax.axis_size("seq")
    n_sub = lax.axis_size("sub")
    heads_here = QH // n_seq
    group = QH // KVH
    query_local = lax.all_to_all(query_rows, "seq", split_axis=2, concat_axis=1, tiled=True)
    key_full, value_full = (
        lax.all_gather(key_rows, "seq", axis=1, tiled=True),
        lax.all_gather(value_rows, "seq", axis=1, tiled=True),
    )
    first_head = lax.axis_index("seq") * heads_here
    key_list = []
    value_list = []
    for head in range(heads_here):
        kv_start = (first_head + head) // group * HD
        key_list.append(lax.dynamic_slice_in_dim(key_full[0], kv_start, HD, 1))
        value_list.append(lax.dynamic_slice_in_dim(value_full[0], kv_start, HD, 1))
    length = query_local.shape[1]
    block = min(length, max(512, length // 8))
    outputs = [
        attend_head(
            query_local[0, :, head * HD : (head + 1) * HD], key_list[head], value_list[head], block
        )
        for head in range(heads_here)
    ]
    head_block = jnp.concatenate(outputs, axis=1)[None]
    attended = lax.all_to_all(head_block, "seq", split_axis=1, concat_axis=2, tiled=True)[0]
    projected = jnp.dot(
        attended,
        lax.all_gather(out_proj, "seq", axis=0, tiled=True),
        preferred_element_type=jnp.float32,
    )
    hidden = (residual_in[0].astype(jnp.float32) + projected).astype(jnp.bfloat16)
    wide = hidden.astype(jnp.float32)
    normed = (
        wide
        * lax.rsqrt(jnp.mean(wide * wide, axis=1, keepdims=True) + 1e-06)
        * norm_gain.astype(jnp.float32)
    ).astype(jnp.bfloat16)
    topk = expert_ids.shape[2]
    experts = n_seq * n_sub
    cap = max(2, (5 * tokens * topk + 4 * experts - 1) // (4 * experts))
    flat_ids = expert_ids[0].reshape(-1)
    items = flat_ids.shape[0]
    ranks = rank_in_expert(flat_ids, experts)
    slot_of = flat_ids * cap + ranks
    slots_out = experts * cap
    item_of_slot = (
        jnp.full((slots_out,), items, jnp.int32).at[slot_of].set(jnp.arange(items, dtype=jnp.int32))
    )
    padded_rows = jnp.concatenate([normed, jnp.zeros((1, D), jnp.bfloat16)], axis=0)
    padded_gates = jnp.concatenate(
        [gate_weights[0].reshape(-1), jnp.zeros((1,), jnp.bfloat16)], axis=0
    )
    token_of_slot = jnp.where(item_of_slot < items, item_of_slot // topk, tokens)
    send_rows = padded_rows[token_of_slot].reshape(experts, cap, D)
    send_gates = padded_gates[item_of_slot].reshape(experts, cap)
    recv_rows, recv_gates = (
        lax.all_to_all(send_rows, ("seq", "sub"), split_axis=0, concat_axis=0, tiled=True),
        lax.all_to_all(send_gates, ("seq", "sub"), split_axis=0, concat_axis=0, tiled=True),
    )
    slots_in = experts * cap
    valid = recv_gates > 0
    counts = jnp.sum(valid.astype(jnp.int32), axis=1)
    offsets = jnp.cumsum(counts) - counts
    dest = jnp.where(
        valid, offsets[:, None] + jnp.arange(cap, dtype=jnp.int32)[None, :], slots_in
    ).reshape(-1)
    source_of = (
        jnp.full((slots_in + 1,), slots_in, jnp.int32)
        .at[dest]
        .set(jnp.arange(slots_in, dtype=jnp.int32))[:slots_in]
    )
    compact_rows = jnp.concatenate(
        [recv_rows.reshape(slots_in, D), jnp.zeros((1, D), jnp.bfloat16)], axis=0
    )[source_of]
    compact_gates = jnp.concatenate(
        [recv_gates.reshape(-1), jnp.zeros((1,), jnp.bfloat16)], axis=0
    )[source_of].astype(jnp.float32)
    filled = jnp.sum(counts)
    n_blocks = (filled + slots_in - 1) // slots_in
    w_gate = expert_gate[0]
    w_up = expert_up[0]
    w_down = expert_down[0]

    def expert_block(index, results):
        gate_proj = jnp.dot(compact_rows, w_gate, preferred_element_type=jnp.float32)
        up_proj = jnp.dot(compact_rows, w_up, preferred_element_type=jnp.float32)
        inner = (jax.nn.silu(gate_proj) * up_proj).astype(jnp.bfloat16)
        weighted = (
            jnp.dot(inner, w_down, preferred_element_type=jnp.float32) * compact_gates[:, None]
        )
        return weighted.astype(jnp.bfloat16)

    results = lax.fori_loop(0, n_blocks, expert_block, jnp.zeros((slots_in, D), jnp.bfloat16))
    returned = jnp.concatenate([results, jnp.zeros((1, D), jnp.bfloat16)], axis=0)[dest].reshape(
        experts, cap, D
    )
    back = lax.all_to_all(
        returned, ("seq", "sub"), split_axis=0, concat_axis=0, tiled=True
    ).reshape(slots_out, D)
    gathered = back[slot_of].reshape(tokens, topk, D).astype(jnp.float32)
    mixture = jnp.sum(gathered, axis=1)
    return (wide + mixture).astype(jnp.bfloat16)[None]


def attend_project_kernel(heads, q_ref, k_ref, v_ref, w_ref, o_ref):
    block = q_ref.shape[0]
    length = k_ref.shape[0]
    start = pl.program_id(0) * block
    row_pos = start + lax.broadcasted_iota(jnp.int32, (block, length), 0)
    col_pos = lax.broadcasted_iota(jnp.int32, (block, length), 1)
    allowed = row_pos >= col_pos
    scale = 1.0 / HD**0.5
    outs = []
    for head in range(heads):
        q = q_ref[:, head * HD : (head + 1) * HD]
        scores = (
            lax.dot_general(
                q, k_ref[...], (((1,), (1,)), ((), ())), preferred_element_type=jnp.float32
            )
            * scale
        )
        scores = jnp.where(allowed, scores, -1e30)
        weights = jnp.exp(scores - jnp.max(scores, axis=1, keepdims=True))
        total = jnp.sum(weights, axis=1, keepdims=True)
        probs = (weights * (1.0 / total)).astype(jnp.bfloat16)
        outs.append(
            jnp.dot(probs, v_ref[...], preferred_element_type=jnp.float32).astype(jnp.bfloat16)
        )
    attended = jnp.concatenate(outs, axis=1)
    o_ref[...] = jnp.dot(attended, w_ref[...], preferred_element_type=jnp.float32).astype(
        o_ref.dtype
    )


def attend_project(queries, keys, values, weights):
    length = queries.shape[0]
    block = min(128, length)
    width = queries.shape[1]
    return pl.pallas_call(
        functools.partial(attend_project_kernel, width // HD),
        grid=(length // block,),
        in_specs=[
            pl.BlockSpec((block, width), lambda i: (i, 0)),
            pl.BlockSpec((length, HD), lambda i: (0, 0)),
            pl.BlockSpec((length, HD), lambda i: (0, 0)),
            pl.BlockSpec(weights.shape, lambda i: (0, 0)),
        ],
        out_specs=pl.BlockSpec((block, weights.shape[1]), lambda i: (i, 0)),
        out_shape=jax.ShapeDtypeStruct((length, weights.shape[1]), jnp.bfloat16),
        name="attend_project",
    )(queries, keys, values, weights)


def expert_kernel(x_ref, c_ref, wg_ref, wu_ref, wd_ref, o_ref):
    x = x_ref[...]
    gate = jnp.dot(x, wg_ref[...], preferred_element_type=jnp.float32)
    up = jnp.dot(x, wu_ref[...], preferred_element_type=jnp.float32)
    inner = (gate / (1.0 + jnp.exp(-gate)) * up).astype(jnp.bfloat16)
    out = jnp.dot(inner, wd_ref[...], preferred_element_type=jnp.float32)
    o_ref[...] = (out * c_ref[...]).astype(jnp.bfloat16)


def expert_rows(rows, coeffs, w_gate, w_up, w_down):
    count, width = rows.shape
    block = 256
    return pl.pallas_call(
        expert_kernel,
        grid=(count // block,),
        in_specs=[
            pl.BlockSpec((block, width), lambda i: (i, 0)),
            pl.BlockSpec((block, 1), lambda i: (i, 0)),
            pl.BlockSpec(w_gate.shape, lambda i: (0, 0), pipeline_mode=pl.Buffered(1)),
            pl.BlockSpec(w_up.shape, lambda i: (0, 0), pipeline_mode=pl.Buffered(1)),
            pl.BlockSpec(w_down.shape, lambda i: (0, 0), pipeline_mode=pl.Buffered(1)),
        ],
        out_specs=pl.BlockSpec((block, width), lambda i: (i, 0)),
        out_shape=jax.ShapeDtypeStruct((count, width), jnp.bfloat16),
        name="expert_rows",
    )(rows, coeffs, w_gate, w_up, w_down)


def per_device_dense(
    query_rows,
    key_rows,
    value_rows,
    residual_in,
    out_proj,
    norm_gain,
    expert_ids,
    gate_weights,
    expert_gate,
    expert_up,
    expert_down,
):
    n_seq = lax.axis_size("seq")
    n_sub = lax.axis_size("sub")
    experts = n_seq * n_sub
    heads_here = QH // n_seq
    group = QH // KVH
    chosen = expert_ids[0][:, :, None] == jnp.arange(experts, dtype=jnp.int32)[None, None, :]
    coeffs_local = jnp.sum(
        jnp.where(chosen, gate_weights[0].astype(jnp.float32)[:, :, None], 0.0), axis=1
    ).astype(jnp.bfloat16)
    coeffs_all = lax.all_gather(coeffs_local, ("seq", "sub"), axis=0, tiled=True)
    my_expert = lax.axis_index("seq") * n_sub + lax.axis_index("sub")
    coeffs = lax.dynamic_slice_in_dim(coeffs_all, my_expert, 1, 1).astype(jnp.float32)

    query_local = lax.all_to_all(query_rows[0], "seq", split_axis=1, concat_axis=0, tiled=True)
    key_values = lax.all_gather(
        jnp.concatenate([key_rows[0], value_rows[0]], axis=1), "seq", axis=0, tiled=True
    )
    kv_start = lax.axis_index("seq") * heads_here // group * HD
    keys = lax.dynamic_slice_in_dim(key_values, kv_start, HD, 1)
    values = lax.dynamic_slice_in_dim(key_values, KVH * HD + kv_start, HD, 1)
    partial = attend_project(query_local, keys, values, out_proj)
    projected = lax.psum_scatter(partial, "seq", scatter_dimension=0, tiled=True)
    hidden = (residual_in[0].astype(jnp.float32) + projected.astype(jnp.float32)).astype(
        jnp.bfloat16
    )
    wide = hidden.astype(jnp.float32)
    normed = (
        wide
        * lax.rsqrt(jnp.mean(wide * wide, axis=1, keepdims=True) + 1e-06)
        * norm_gain.astype(jnp.float32)
    ).astype(jnp.bfloat16)
    rows = lax.all_gather(normed, ("seq", "sub"), axis=0, tiled=True)
    results = expert_rows(rows, coeffs, expert_gate[0], expert_up[0], expert_down[0])
    mixture = lax.psum_scatter(results, ("seq", "sub"), scatter_dimension=0, tiled=True)
    return (wide + mixture.astype(jnp.float32)).astype(jnp.bfloat16)[None]


def per_device(*args):
    tokens = args[0].shape[1]
    topk = args[6].shape[2]
    n_seq = lax.axis_size("seq")
    experts = n_seq * lax.axis_size("sub")
    cap = max(2, (5 * tokens * topk + 4 * experts - 1) // (4 * experts))
    if 2 * cap >= tokens and QH // n_seq <= QH // KVH:
        return per_device_dense(*args)
    return per_device_routed(*args)


def solution(mesh):
    placed = (
        P(("grp", "sub"), "seq", None),
        P(("grp", "sub"), "seq", None),
        P(("grp", "sub"), "seq", None),
        P(("grp", "sub"), "seq", None),
        P("seq", None),
        P(),
        P(("grp", "sub"), "seq", None),
        P(("grp", "sub"), "seq", None),
        P(("seq", "sub"), None, None),
        P(("seq", "sub"), None, None),
        P(("seq", "sub"), None, None),
    )
    return jax.shard_map(
        per_device,
        mesh=mesh,
        in_specs=placed,
        out_specs=P(("grp", "sub"), "seq", None),
        check_vma=False,
    )
```

```python
import functools
import jax
import jax.numpy as jnp
from jax import lax
from jax.experimental import pallas as pl
from jax.experimental.pallas import tpu as pltpu
from jax.sharding import PartitionSpec as P

D = 2048
HD = 128
QH = 16
KVH = 2


def attend_head(queries, keys_one, values_one, block):
    length = queries.shape[0]
    scale = 1.0 / queries.shape[1] ** 0.5
    pieces = []
    for part_index in range(length // block):
        stop = (part_index + 1) * block
        rows_here = queries[part_index * block : stop]
        scores = (
            jnp.einsum("qd,kd->qk", rows_here, keys_one[:stop], preferred_element_type=jnp.float32)
            * scale
        )
        row_pos = part_index * block + jnp.arange(block, dtype=jnp.int32)
        col_pos = jnp.arange(stop, dtype=jnp.int32)
        scores = jnp.where(row_pos[:, None] >= col_pos[None, :], scores, -1e30)
        peak = jnp.max(scores, axis=1, keepdims=True)
        weights = jnp.exp(scores - peak)
        probs = (weights / jnp.sum(weights, axis=1, keepdims=True)).astype(jnp.bfloat16)
        pieces.append(
            jnp.dot(probs, values_one[:stop], preferred_element_type=jnp.float32).astype(
                jnp.bfloat16
            )
        )
    return jnp.concatenate(pieces, axis=0)


def rank_in_expert(flat_ids, experts):
    items = flat_ids.shape[0]
    width = 128
    n_parts = items // width
    onehot = (
        (flat_ids[:, None] == jnp.arange(experts, dtype=jnp.int32)[None, :])
        .astype(jnp.bfloat16)
        .reshape(n_parts, width, experts)
    )
    lower = (
        jnp.arange(width, dtype=jnp.int32)[:, None] > jnp.arange(width, dtype=jnp.int32)[None, :]
    ).astype(jnp.bfloat16)
    within = jnp.einsum("ij,bje->bie", lower, onehot, preferred_element_type=jnp.float32)
    part_counts = jnp.sum(onehot.astype(jnp.float32), axis=1)
    earlier = jnp.cumsum(part_counts, axis=0) - part_counts
    ranks = jnp.sum((within + earlier[:, None, :]) * onehot.astype(jnp.float32), axis=2)
    return ranks.reshape(items).astype(jnp.int32)


def per_device_routed(
    query_rows,
    key_rows,
    value_rows,
    residual_in,
    out_proj,
    norm_gain,
    expert_ids,
    gate_weights,
    expert_gate,
    expert_up,
    expert_down,
):
    tokens = query_rows.shape[1]
    n_seq = lax.axis_size("seq")
    n_sub = lax.axis_size("sub")
    heads_here = QH // n_seq
    group = QH // KVH
    query_local = lax.all_to_all(query_rows, "seq", split_axis=2, concat_axis=1, tiled=True)
    key_full, value_full = (
        lax.all_gather(key_rows, "seq", axis=1, tiled=True),
        lax.all_gather(value_rows, "seq", axis=1, tiled=True),
    )
    first_head = lax.axis_index("seq") * heads_here
    key_list = []
    value_list = []
    for head in range(heads_here):
        kv_start = (first_head + head) // group * HD
        key_list.append(lax.dynamic_slice_in_dim(key_full[0], kv_start, HD, 1))
        value_list.append(lax.dynamic_slice_in_dim(value_full[0], kv_start, HD, 1))
    length = query_local.shape[1]
    block = min(length, max(512, length // 8))
    outputs = [
        attend_head(
            query_local[0, :, head * HD : (head + 1) * HD], key_list[head], value_list[head], block
        )
        for head in range(heads_here)
    ]
    head_block = jnp.concatenate(outputs, axis=1)[None]
    attended = lax.all_to_all(head_block, "seq", split_axis=1, concat_axis=2, tiled=True)[0]
    projected = jnp.dot(
        attended,
        lax.all_gather(out_proj, "seq", axis=0, tiled=True),
        preferred_element_type=jnp.float32,
    )
    hidden = (residual_in[0].astype(jnp.float32) + projected).astype(jnp.bfloat16)
    wide = hidden.astype(jnp.float32)
    normed = (
        wide
        * lax.rsqrt(jnp.mean(wide * wide, axis=1, keepdims=True) + 1e-06)
        * norm_gain.astype(jnp.float32)
    ).astype(jnp.bfloat16)
    topk = expert_ids.shape[2]
    experts = n_seq * n_sub
    cap = max(2, (5 * tokens * topk + 4 * experts - 1) // (4 * experts))
    flat_ids = expert_ids[0].reshape(-1)
    items = flat_ids.shape[0]
    ranks = rank_in_expert(flat_ids, experts)
    slot_of = flat_ids * cap + ranks
    slots_out = experts * cap
    item_of_slot = (
        jnp.full((slots_out,), items, jnp.int32).at[slot_of].set(jnp.arange(items, dtype=jnp.int32))
    )
    padded_rows = jnp.concatenate([normed, jnp.zeros((1, D), jnp.bfloat16)], axis=0)
    padded_gates = jnp.concatenate(
        [gate_weights[0].reshape(-1), jnp.zeros((1,), jnp.bfloat16)], axis=0
    )
    token_of_slot = jnp.where(item_of_slot < items, item_of_slot // topk, tokens)
    send_rows = padded_rows[token_of_slot].reshape(experts, cap, D)
    send_gates = padded_gates[item_of_slot].reshape(experts, cap)
    recv_rows, recv_gates = (
        lax.all_to_all(send_rows, ("seq", "sub"), split_axis=0, concat_axis=0, tiled=True),
        lax.all_to_all(send_gates, ("seq", "sub"), split_axis=0, concat_axis=0, tiled=True),
    )
    slots_in = experts * cap
    valid = recv_gates > 0
    counts = jnp.sum(valid.astype(jnp.int32), axis=1)
    offsets = jnp.cumsum(counts) - counts
    dest = jnp.where(
        valid, offsets[:, None] + jnp.arange(cap, dtype=jnp.int32)[None, :], slots_in
    ).reshape(-1)
    source_of = (
        jnp.full((slots_in + 1,), slots_in, jnp.int32)
        .at[dest]
        .set(jnp.arange(slots_in, dtype=jnp.int32))[:slots_in]
    )
    compact_rows = jnp.concatenate(
        [recv_rows.reshape(slots_in, D), jnp.zeros((1, D), jnp.bfloat16)], axis=0
    )[source_of]
    compact_gates = jnp.concatenate(
        [recv_gates.reshape(-1), jnp.zeros((1,), jnp.bfloat16)], axis=0
    )[source_of].astype(jnp.float32)
    filled = jnp.sum(counts)
    n_blocks = (filled + slots_in - 1) // slots_in
    w_gate = expert_gate[0]
    w_up = expert_up[0]
    w_down = expert_down[0]

    def expert_block(index, results):
        gate_proj = jnp.dot(compact_rows, w_gate, preferred_element_type=jnp.float32)
        up_proj = jnp.dot(compact_rows, w_up, preferred_element_type=jnp.float32)
        inner = (jax.nn.silu(gate_proj) * up_proj).astype(jnp.bfloat16)
        weighted = (
            jnp.dot(inner, w_down, preferred_element_type=jnp.float32) * compact_gates[:, None]
        )
        return weighted.astype(jnp.bfloat16)

    results = lax.fori_loop(0, n_blocks, expert_block, jnp.zeros((slots_in, D), jnp.bfloat16))
    returned = jnp.concatenate([results, jnp.zeros((1, D), jnp.bfloat16)], axis=0)[dest].reshape(
        experts, cap, D
    )
    back = lax.all_to_all(
        returned, ("seq", "sub"), split_axis=0, concat_axis=0, tiled=True
    ).reshape(slots_out, D)
    gathered = back[slot_of].reshape(tokens, topk, D).astype(jnp.float32)
    mixture = jnp.sum(gathered, axis=1)
    return (wide + mixture).astype(jnp.bfloat16)[None]


def attend_project_kernel(heads, q_ref, k_ref, v_ref, w_ref, o_ref):
    block = q_ref.shape[0]
    length = k_ref.shape[0]
    start = pl.program_id(0) * block
    row_pos = start + lax.broadcasted_iota(jnp.int32, (block, length), 0)
    col_pos = lax.broadcasted_iota(jnp.int32, (block, length), 1)
    allowed = row_pos >= col_pos
    scale = 1.0 / HD**0.5
    outs = []
    for head in range(heads):
        q = q_ref[:, head * HD : (head + 1) * HD]
        scores = (
            lax.dot_general(
                q, k_ref[...], (((1,), (1,)), ((), ())), preferred_element_type=jnp.float32
            )
            * scale
        )
        scores = jnp.where(allowed, scores, -1e30)
        weights = jnp.exp(scores - jnp.max(scores, axis=1, keepdims=True))
        total = jnp.sum(weights, axis=1, keepdims=True)
        probs = (weights * (1.0 / total)).astype(jnp.bfloat16)
        outs.append(
            jnp.dot(probs, v_ref[...], preferred_element_type=jnp.float32).astype(jnp.bfloat16)
        )
    attended = jnp.concatenate(outs, axis=1)
    o_ref[...] = jnp.dot(attended, w_ref[...], preferred_element_type=jnp.float32).astype(
        o_ref.dtype
    )


def attend_project(queries, keys, values, weights):
    length = queries.shape[0]
    block = min(128, length)
    width = queries.shape[1]
    return pl.pallas_call(
        functools.partial(attend_project_kernel, width // HD),
        grid=(length // block,),
        in_specs=[
            pl.BlockSpec((block, width), lambda i: (i, 0)),
            pl.BlockSpec((length, HD), lambda i: (0, 0)),
            pl.BlockSpec((length, HD), lambda i: (0, 0)),
            pl.BlockSpec(weights.shape, lambda i: (0, 0)),
        ],
        out_specs=pl.BlockSpec((block, weights.shape[1]), lambda i: (i, 0)),
        out_shape=jax.ShapeDtypeStruct((length, weights.shape[1]), jnp.bfloat16),
        name="attend_project",
    )(queries, keys, values, weights)


def nearest_order(n):
    return [sorted(range(n), key=lambda p: (abs(p - z), p)) for z in range(n)]


def lookup(table, i, j):
    total = 0
    for a, row in enumerate(table):
        for b, value in enumerate(row):
            if value:
                hit = jnp.logical_and(i == a, j == b)
                total = total + jnp.where(hit, value, 0)
    return total


def experts_kernel(
    n_sub,
    x_hbm,
    wide_ref,
    wg_hbm,
    wu_hbm,
    wd_hbm,
    o_ref,
    rows,
    outs,
    from_core,
    from_y,
    from_low,
    from_high,
    wg,
    wu,
    wd,
    load_sem,
    row_recv,
    up_send,
    down_send,
    y_send,
    core_send,
    relay_send,
    core_recv,
    result_send,
    y_recv,
    result_y_send,
    low_recv,
    high_recv,
    result_up_send,
    result_down_send,
):
    seq = lax.axis_index("seq")
    z = lax.axis_index("sub")
    y = seq // 2
    c = seq % 2
    tokens = wide_ref.shape[0]
    width = wide_ref.shape[1]
    half = tokens // 2
    order = nearest_order(n_sub)
    me = seq * n_sub + z
    high = {"sub": z + 1}
    low = {"sub": z - 1}
    across = {"seq": (1 - y) * 2 + c}
    partner = {"seq": y * 2 + 1 - c}
    has_high = z < n_sub - 1
    has_low = z > 0

    def slot(yy, p, cc):
        return (yy * n_sub + p) * 2 + cc

    def piece(ref, index, h):
        return ref.at[pl.ds(pl.multiple_of(index * tokens + h * half, half), half), :]

    def remote(src, dst, send, recv, target):
        return pltpu.make_async_remote_copy(
            src_ref=src,
            dst_ref=dst,
            send_sem=send,
            recv_sem=recv,
            device_id=target,
            device_id_type=pl.DeviceIdType.MESH,
        )

    loads = [
        pltpu.make_async_copy(x_hbm, rows.at[pl.ds(pl.multiple_of(slot(y, z, c) * tokens, tokens), tokens), :], load_sem.at[0]),
        pltpu.make_async_copy(wg_hbm, wg, load_sem.at[1]),
        pltpu.make_async_copy(wu_hbm, wu, load_sem.at[2]),
        pltpu.make_async_copy(wd_hbm, wd, load_sem.at[3]),
    ]
    for load in loads:
        load.start()

    barrier = pltpu.get_barrier_semaphore()
    pl.semaphore_signal(barrier, 1, device_id=across, device_id_type=pl.DeviceIdType.MESH)
    pl.semaphore_signal(barrier, 1, device_id=partner, device_id_type=pl.DeviceIdType.MESH)

    @pl.when(has_high)
    def _():
        pl.semaphore_signal(barrier, 1, device_id=high, device_id_type=pl.DeviceIdType.MESH)

    @pl.when(has_low)
    def _():
        pl.semaphore_signal(barrier, 1, device_id=low, device_id_type=pl.DeviceIdType.MESH)

    peers = 2 + jnp.where(has_high, 1, 0) + jnp.where(has_low, 1, 0)
    pl.semaphore_wait(barrier, peers)

    loads[0].wait()

    def row_copy(index, h, send, target):
        here = piece(rows, index, h)
        return remote(here, here, send, row_recv.at[index * 2 + h], target)

    def wait_rows(index, h):
        row_copy(index, h, relay_send.at[0], partner).wait_recv()

    def column_copies(p, h):
        index = slot(y, p, c)
        at = p * 2 + h
        return (
            (jnp.logical_and(p <= z, has_high), row_copy(index, h, up_send.at[at], high)),
            (jnp.logical_and(p >= z, has_low), row_copy(index, h, down_send.at[at], low)),
            (None, row_copy(index, h, y_send.at[at], across)),
            (None, row_copy(index, h, core_send.at[at], partner)),
        )

    def spread(p, h):
        for condition, copy in column_copies(p, h):
            if condition is None:
                copy.start()
            else:

                @pl.when(condition)
                def _():
                    copy.start()

    def relay_copy(p, h):
        return row_copy(slot(1 - y, p, c), h, relay_send.at[p * 2 + h], partner)

    def result_copy(yy, p):
        index = slot(yy, p, 1 - c)
        pair = yy * n_sub + p
        src = outs.at[pl.ds(pl.multiple_of(index * tokens, tokens), tokens), :]
        dst = from_core.at[pl.ds(pl.multiple_of(pair * tokens, tokens), tokens), :]
        return remote(src, dst, result_send.at[pair], core_recv.at[pair], partner)

    def compute(yy, p):
        wait_rows(slot(yy, p, 1 - c), 0)
        wait_rows(slot(yy, p, 1 - c), 1)
        at = pl.ds(pl.multiple_of((yy * n_sub + p) * 2 * tokens, 2 * tokens), 2 * tokens)
        x = rows[at, :width]
        gains = rows[at, width:].astype(jnp.float32)
        lane = lax.broadcasted_iota(jnp.int32, gains.shape, 1)
        coeff = jnp.sum(jnp.where(lane == me, gains, 0.0), axis=1, keepdims=True)
        gate = jnp.dot(x, wg[...], preferred_element_type=jnp.float32)
        up = jnp.dot(x, wu[...], preferred_element_type=jnp.float32)
        inner = (gate / (1.0 + jnp.exp(-gate)) * up).astype(jnp.bfloat16)
        out = jnp.dot(inner, wd[...], preferred_element_type=jnp.float32)
        outs[at, :] = (out * coeff).astype(jnp.bfloat16)
        result_copy(yy, p).start()

    def gather_step(k, carry):
        t = k // 2
        other = k % 2

        @pl.when(other == 0)
        def _():
            p = lookup(order, z, t)

            @pl.when(t > 0)
            def _():
                wait_rows(slot(y, p, c), 0)

            spread(p, 0)

            @pl.when(t > 0)
            def _():
                wait_rows(slot(y, p, c), 1)

            spread(p, 1)

        @pl.when(k == 0)
        def _():
            for load in loads[1:]:
                load.wait()

        p = lookup(order, z, t)

        @pl.when(other == 1)
        def _():
            wait_rows(slot(1 - y, p, c), 0)
            relay_copy(p, 0).start()
            wait_rows(slot(1 - y, p, c), 1)
            relay_copy(p, 1).start()

        compute(jnp.where(other == 1, 1 - y, y), p)
        return carry

    lax.fori_loop(0, 2 * n_sub, gather_step, 0)

    def wide_load(ref, index, h):
        at = pl.ds(pl.multiple_of(index * tokens + h * half, half), half)
        return ref[at, :].astype(jnp.float32)

    def y_copy(p, h):
        at = p * 2 + h
        return remote(
            piece(outs, slot(1 - y, p, c), h),
            piece(from_y, p, h),
            result_y_send.at[at],
            y_recv.at[at],
            across,
        )

    def z_copy(p, h, buffer, send, recv, target):
        at = p * 2 + h
        return remote(
            piece(outs, slot(y, p, c), h), piece(buffer, p, h), send.at[at], recv.at[at], target
        )

    def up_copy(p, h):
        return z_copy(p, h, from_low, result_up_send, low_recv, high)

    def down_copy(p, h):
        return z_copy(p, h, from_high, result_down_send, high_recv, low)

    def store_out(index, h, value):
        at = pl.ds(pl.multiple_of(index * tokens + h * half, half), half)
        outs[at, :] = value.astype(jnp.bfloat16)

    def y_step(k, carry):
        p = lookup(order, z, n_sub - 1 - k)
        result_copy(1 - y, p).wait_recv()
        index = slot(1 - y, p, c)
        for h in range(2):
            store_out(
                index, h, wide_load(outs, index, h) + wide_load(from_core, (1 - y) * n_sub + p, h)
            )
            y_copy(p, h).start()
        return carry

    lax.fori_loop(0, n_sub, y_step, 0)

    def own_step(k, carry):
        p = lookup(order, z, n_sub - 1 - k)
        result_copy(y, p).wait_recv()
        index = slot(y, p, c)
        store = wide_load(outs, index, 0) + wide_load(from_core, y * n_sub + p, 0)
        store_out(index, 0, store)
        store = wide_load(outs, index, 1) + wide_load(from_core, y * n_sub + p, 1)
        store_out(index, 1, store)
        return carry

    lax.fori_loop(0, n_sub, own_step, 0)

    def z_step(k, carry):
        p = lookup(order, z, n_sub - 1 - k // 2)
        h = k % 2
        index = slot(y, p, c)
        y_copy(p, h).wait_recv()

        @pl.when(p > z)
        def _():
            store_out(index, h, wide_load(outs, index, h) + wide_load(from_y, p, h))

            @pl.when(has_low)
            def _():
                up_copy(p, h).wait_recv()
                store_out(index, h, wide_load(outs, index, h) + wide_load(from_low, p, h))

            up_copy(p, h).start()

        @pl.when(p < z)
        def _():
            store_out(index, h, wide_load(outs, index, h) + wide_load(from_y, p, h))

            @pl.when(has_high)
            def _():
                down_copy(p, h).wait_recv()
                store_out(index, h, wide_load(outs, index, h) + wide_load(from_high, p, h))

            down_copy(p, h).start()

        @pl.when(p == z)
        def _():
            at = pl.ds(pl.multiple_of(h * half, half), half)
            store_out(index, h, wide_load(outs, index, h) + wide_load(from_y, p, h))

            @pl.when(has_low)
            def _():
                up_copy(p, h).wait_recv()
                store_out(index, h, wide_load(outs, index, h) + wide_load(from_low, p, h))

            @pl.when(has_high)
            def _():
                down_copy(p, h).wait_recv()
                store_out(index, h, wide_load(outs, index, h) + wide_load(from_high, p, h))

            o_ref[at, :] = (wide_ref[at, :].astype(jnp.float32) + wide_load(outs, index, h)).astype(
                jnp.bfloat16
            )

        return carry

    lax.fori_loop(0, 2 * n_sub, z_step, 0)

    def drain(k, carry):
        p = k // 2
        h = k % 2
        for condition, copy in column_copies(p, h):
            if condition is None:
                copy.wait_send()
            else:

                @pl.when(condition)
                def _():
                    copy.wait_send()

        relay_copy(p, h).wait_send()
        y_copy(p, h).wait_send()
        result_copy(h, p).wait_send()

        @pl.when(p > z)
        def _():
            up_copy(p, h).wait_send()

        @pl.when(p < z)
        def _():
            down_copy(p, h).wait_send()

        return carry

    lax.fori_loop(0, 2 * n_sub, drain, 0)


def experts_exchange(rows_ext, hidden, w_gate, w_up, w_down, n_sub):
    tokens, width = hidden.shape
    blocks = 4 * n_sub
    dma = lambda count: pltpu.SemaphoreType.DMA((count,))
    any_spec = pl.BlockSpec(memory_space=pl.ANY)
    vmem_spec = pl.BlockSpec(memory_space=pltpu.VMEM)
    bf = jnp.bfloat16
    return pl.pallas_call(
        functools.partial(experts_kernel, n_sub),
        in_specs=[any_spec, vmem_spec, any_spec, any_spec, any_spec],
        out_specs=vmem_spec,
        out_shape=jax.ShapeDtypeStruct((tokens, width), bf),
        scratch_shapes=[
            pltpu.VMEM((blocks * tokens, rows_ext.shape[1]), bf),
            pltpu.VMEM((blocks * tokens, width), bf),
            pltpu.VMEM((2 * n_sub * tokens, width), bf),
            pltpu.VMEM((n_sub * tokens, width), bf),
            pltpu.VMEM((n_sub * tokens, width), bf),
            pltpu.VMEM((n_sub * tokens, width), bf),
            pltpu.VMEM(w_gate.shape, bf),
            pltpu.VMEM(w_up.shape, bf),
            pltpu.VMEM(w_down.shape, bf),
            dma(4),
            dma(2 * blocks),
            dma(2 * n_sub),
            dma(2 * n_sub),
            dma(2 * n_sub),
            dma(2 * n_sub),
            dma(2 * n_sub),
            dma(2 * n_sub),
            dma(2 * n_sub),
            dma(2 * n_sub),
            dma(2 * n_sub),
            dma(2 * n_sub),
            dma(2 * n_sub),
            dma(2 * n_sub),
            dma(2 * n_sub),
        ],
        compiler_params=pltpu.CompilerParams(
            collective_id=0, has_side_effects=True, vmem_limit_bytes=60 * 2**20
        ),
        name="experts_exchange",
    )(rows_ext, hidden, w_gate, w_up, w_down)


def per_device_dense(
    query_rows,
    key_rows,
    value_rows,
    residual_in,
    out_proj,
    norm_gain,
    expert_ids,
    gate_weights,
    expert_gate,
    expert_up,
    expert_down,
):
    n_seq = lax.axis_size("seq")
    n_sub = lax.axis_size("sub")
    experts = n_seq * n_sub
    heads_here = QH // n_seq
    group = QH // KVH
    chosen = expert_ids[0][:, :, None] == jnp.arange(experts, dtype=jnp.int32)[None, None, :]
    coeffs_local = jnp.sum(
        jnp.where(chosen, gate_weights[0].astype(jnp.float32)[:, :, None], 0.0), axis=1
    ).astype(jnp.bfloat16)

    query_local = lax.all_to_all(query_rows[0], "seq", split_axis=1, concat_axis=0, tiled=True)
    key_values = lax.all_gather(
        jnp.concatenate([key_rows[0], value_rows[0]], axis=1), "seq", axis=0, tiled=True
    )
    kv_start = lax.axis_index("seq") * heads_here // group * HD
    keys = lax.dynamic_slice_in_dim(key_values, kv_start, HD, 1)
    values = lax.dynamic_slice_in_dim(key_values, KVH * HD + kv_start, HD, 1)
    partial = attend_project(query_local, keys, values, out_proj)
    projected = lax.psum_scatter(partial, "seq", scatter_dimension=0, tiled=True)
    hidden = (residual_in[0].astype(jnp.float32) + projected.astype(jnp.float32)).astype(
        jnp.bfloat16
    )
    wide = hidden.astype(jnp.float32)
    normed = (
        wide
        * lax.rsqrt(jnp.mean(wide * wide, axis=1, keepdims=True) + 1e-06)
        * norm_gain.astype(jnp.float32)
    ).astype(jnp.bfloat16)
    lanes = 128 * ((experts + 127) // 128)
    rows_ext = jnp.concatenate(
        [normed, jnp.pad(coeffs_local, ((0, 0), (0, lanes - experts)))], axis=1
    )
    return experts_exchange(
        rows_ext, hidden, expert_gate[0], expert_up[0], expert_down[0], n_sub
    )[None]


def per_device(*args):
    tokens = args[0].shape[1]
    topk = args[6].shape[2]
    n_seq = lax.axis_size("seq")
    experts = n_seq * lax.axis_size("sub")
    cap = max(2, (5 * tokens * topk + 4 * experts - 1) // (4 * experts))
    if 2 * cap >= tokens and n_seq == 4:
        return per_device_dense(*args)
    return per_device_routed(*args)


def solution(mesh):
    placed = (
        P(("grp", "sub"), "seq", None),
        P(("grp", "sub"), "seq", None),
        P(("grp", "sub"), "seq", None),
        P(("grp", "sub"), "seq", None),
        P("seq", None),
        P(),
        P(("grp", "sub"), "seq", None),
        P(("grp", "sub"), "seq", None),
        P(("seq", "sub"), None, None),
        P(("seq", "sub"), None, None),
        P(("seq", "sub"), None, None),
    )
    return jax.shard_map(
        per_device,
        mesh=mesh,
        in_specs=placed,
        out_specs=P(("grp", "sub"), "seq", None),
        check_vma=False,
    )
```

```python
import functools
import jax
import jax.numpy as jnp
from jax import lax
from jax.experimental import pallas as pl
from jax.experimental.pallas import tpu as pltpu
from jax.sharding import PartitionSpec as P

D = 2048
HD = 128
QH = 16
KVH = 2


def attend_head(queries, keys_one, values_one, block):
    length = queries.shape[0]
    scale = 1.0 / queries.shape[1] ** 0.5
    pieces = []
    for part_index in range(length // block):
        stop = (part_index + 1) * block
        rows_here = queries[part_index * block : stop]
        scores = (
            jnp.einsum("qd,kd->qk", rows_here, keys_one[:stop], preferred_element_type=jnp.float32)
            * scale
        )
        row_pos = part_index * block + jnp.arange(block, dtype=jnp.int32)
        col_pos = jnp.arange(stop, dtype=jnp.int32)
        scores = jnp.where(row_pos[:, None] >= col_pos[None, :], scores, -1e30)
        peak = jnp.max(scores, axis=1, keepdims=True)
        weights = jnp.exp(scores - peak)
        probs = (weights / jnp.sum(weights, axis=1, keepdims=True)).astype(jnp.bfloat16)
        pieces.append(
            jnp.dot(probs, values_one[:stop], preferred_element_type=jnp.float32).astype(
                jnp.bfloat16
            )
        )
    return jnp.concatenate(pieces, axis=0)


def rank_in_expert(flat_ids, experts):
    items = flat_ids.shape[0]
    width = 128
    n_parts = items // width
    onehot = (
        (flat_ids[:, None] == jnp.arange(experts, dtype=jnp.int32)[None, :])
        .astype(jnp.bfloat16)
        .reshape(n_parts, width, experts)
    )
    lower = (
        jnp.arange(width, dtype=jnp.int32)[:, None] > jnp.arange(width, dtype=jnp.int32)[None, :]
    ).astype(jnp.bfloat16)
    within = jnp.einsum("ij,bje->bie", lower, onehot, preferred_element_type=jnp.float32)
    part_counts = jnp.sum(onehot.astype(jnp.float32), axis=1)
    earlier = jnp.cumsum(part_counts, axis=0) - part_counts
    ranks = jnp.sum((within + earlier[:, None, :]) * onehot.astype(jnp.float32), axis=2)
    return ranks.reshape(items).astype(jnp.int32)


def per_device_routed(
    query_rows,
    key_rows,
    value_rows,
    residual_in,
    out_proj,
    norm_gain,
    expert_ids,
    gate_weights,
    expert_gate,
    expert_up,
    expert_down,
):
    tokens = query_rows.shape[1]
    n_seq = lax.axis_size("seq")
    n_sub = lax.axis_size("sub")
    heads_here = QH // n_seq
    group = QH // KVH
    query_local = lax.all_to_all(query_rows, "seq", split_axis=2, concat_axis=1, tiled=True)
    key_full, value_full = (
        lax.all_gather(key_rows, "seq", axis=1, tiled=True),
        lax.all_gather(value_rows, "seq", axis=1, tiled=True),
    )
    first_head = lax.axis_index("seq") * heads_here
    key_list = []
    value_list = []
    for head in range(heads_here):
        kv_start = (first_head + head) // group * HD
        key_list.append(lax.dynamic_slice_in_dim(key_full[0], kv_start, HD, 1))
        value_list.append(lax.dynamic_slice_in_dim(value_full[0], kv_start, HD, 1))
    length = query_local.shape[1]
    block = min(length, max(512, length // 8))
    outputs = [
        attend_head(
            query_local[0, :, head * HD : (head + 1) * HD], key_list[head], value_list[head], block
        )
        for head in range(heads_here)
    ]
    head_block = jnp.concatenate(outputs, axis=1)[None]
    attended = lax.all_to_all(head_block, "seq", split_axis=1, concat_axis=2, tiled=True)[0]
    projected = jnp.dot(
        attended,
        lax.all_gather(out_proj, "seq", axis=0, tiled=True),
        preferred_element_type=jnp.float32,
    )
    hidden = (residual_in[0].astype(jnp.float32) + projected).astype(jnp.bfloat16)
    wide = hidden.astype(jnp.float32)
    normed = (
        wide
        * lax.rsqrt(jnp.mean(wide * wide, axis=1, keepdims=True) + 1e-06)
        * norm_gain.astype(jnp.float32)
    ).astype(jnp.bfloat16)
    topk = expert_ids.shape[2]
    experts = n_seq * n_sub
    cap = max(2, (5 * tokens * topk + 4 * experts - 1) // (4 * experts))
    flat_ids = expert_ids[0].reshape(-1)
    items = flat_ids.shape[0]
    ranks = rank_in_expert(flat_ids, experts)
    slot_of = flat_ids * cap + ranks
    slots_out = experts * cap
    item_of_slot = (
        jnp.full((slots_out,), items, jnp.int32).at[slot_of].set(jnp.arange(items, dtype=jnp.int32))
    )
    padded_rows = jnp.concatenate([normed, jnp.zeros((1, D), jnp.bfloat16)], axis=0)
    padded_gates = jnp.concatenate(
        [gate_weights[0].reshape(-1), jnp.zeros((1,), jnp.bfloat16)], axis=0
    )
    token_of_slot = jnp.where(item_of_slot < items, item_of_slot // topk, tokens)
    send_rows = padded_rows[token_of_slot].reshape(experts, cap, D)
    send_gates = padded_gates[item_of_slot].reshape(experts, cap)
    recv_rows, recv_gates = (
        lax.all_to_all(send_rows, ("seq", "sub"), split_axis=0, concat_axis=0, tiled=True),
        lax.all_to_all(send_gates, ("seq", "sub"), split_axis=0, concat_axis=0, tiled=True),
    )
    slots_in = experts * cap
    valid = recv_gates > 0
    counts = jnp.sum(valid.astype(jnp.int32), axis=1)
    offsets = jnp.cumsum(counts) - counts
    dest = jnp.where(
        valid, offsets[:, None] + jnp.arange(cap, dtype=jnp.int32)[None, :], slots_in
    ).reshape(-1)
    source_of = (
        jnp.full((slots_in + 1,), slots_in, jnp.int32)
        .at[dest]
        .set(jnp.arange(slots_in, dtype=jnp.int32))[:slots_in]
    )
    compact_rows = jnp.concatenate(
        [recv_rows.reshape(slots_in, D), jnp.zeros((1, D), jnp.bfloat16)], axis=0
    )[source_of]
    compact_gates = jnp.concatenate(
        [recv_gates.reshape(-1), jnp.zeros((1,), jnp.bfloat16)], axis=0
    )[source_of].astype(jnp.float32)
    filled = jnp.sum(counts)
    n_blocks = (filled + slots_in - 1) // slots_in
    w_gate = expert_gate[0]
    w_up = expert_up[0]
    w_down = expert_down[0]

    def expert_block(index, results):
        gate_proj = jnp.dot(compact_rows, w_gate, preferred_element_type=jnp.float32)
        up_proj = jnp.dot(compact_rows, w_up, preferred_element_type=jnp.float32)
        inner = (jax.nn.silu(gate_proj) * up_proj).astype(jnp.bfloat16)
        weighted = (
            jnp.dot(inner, w_down, preferred_element_type=jnp.float32) * compact_gates[:, None]
        )
        return weighted.astype(jnp.bfloat16)

    results = lax.fori_loop(0, n_blocks, expert_block, jnp.zeros((slots_in, D), jnp.bfloat16))
    returned = jnp.concatenate([results, jnp.zeros((1, D), jnp.bfloat16)], axis=0)[dest].reshape(
        experts, cap, D
    )
    back = lax.all_to_all(
        returned, ("seq", "sub"), split_axis=0, concat_axis=0, tiled=True
    ).reshape(slots_out, D)
    gathered = back[slot_of].reshape(tokens, topk, D).astype(jnp.float32)
    mixture = jnp.sum(gathered, axis=1)
    return (wide + mixture).astype(jnp.bfloat16)[None]


def nearest_order(n):
    return [sorted(range(n), key=lambda p: (abs(p - z), p)) for z in range(n)]


def lookup(table, i, j):
    total = 0
    for a, row in enumerate(table):
        for b, value in enumerate(row):
            if value:
                hit = jnp.logical_and(i == a, j == b)
                total = total + jnp.where(hit, value, 0)
    return total


def layer_kernel(
    n_sub,
    q_hbm,
    k_hbm,
    v_hbm,
    residual_ref,
    proj_hbm,
    gain_ref,
    coeff_ref,
    wg_hbm,
    wu_hbm,
    wd_hbm,
    o_ref,
    q_all,
    k_all,
    v_all,
    proj,
    partial,
    core_far,
    core_near,
    across_near,
    wide_ref,
    q_send,
    q_recv,
    kv_send,
    kv_recv,
    part_send,
    part_recv,
    rows,
    outs,
    from_core,
    from_y,
    from_low,
    from_high,
    wg,
    wu,
    wd,
    load_sem,
    row_recv,
    up_send,
    down_send,
    y_send,
    core_send,
    relay_send,
    core_recv,
    result_send,
    y_recv,
    result_y_send,
    low_recv,
    high_recv,
    result_up_send,
    result_down_send,
):
    seq = lax.axis_index("seq")
    z = lax.axis_index("sub")
    y = seq // 2
    c = seq % 2
    tokens = residual_ref.shape[0]
    width = residual_ref.shape[1]
    share = q_all.shape[1]
    heads = share // HD
    length = q_all.shape[0]
    group = QH // KVH
    half = tokens // 2
    order = nearest_order(n_sub)
    me = seq * n_sub + z
    high = {"sub": z + 1}
    low = {"sub": z - 1}
    across = {"seq": (1 - y) * 2 + c}
    partner = {"seq": y * 2 + 1 - c}
    diagonal = {"seq": (1 - y) * 2 + 1 - c}
    has_high = z < n_sub - 1
    has_low = z > 0

    def slot(yy, p, cc):
        return (yy * n_sub + p) * 2 + cc

    def piece(ref, index, h):
        return ref.at[pl.ds(pl.multiple_of(index * tokens + h * half, half), half), :]

    def remote(src, dst, send, recv, target):
        return pltpu.make_async_remote_copy(
            src_ref=src,
            dst_ref=dst,
            send_sem=send,
            recv_sem=recv,
            device_id=target,
            device_id_type=pl.DeviceIdType.MESH,
        )

    def query_part(s):
        return q_hbm.at[:, pl.ds(pl.multiple_of(s * share, share), share)]

    def cache_part(ref, s):
        return ref.at[:, pl.ds(pl.multiple_of(s * heads // group * HD, HD), HD)]

    def token_rows(ref, s):
        return ref.at[pl.ds(pl.multiple_of(s * tokens, tokens), tokens), :]

    own_parts = [
        pltpu.make_async_copy(query_part(seq), token_rows(q_all, seq), load_sem.at[0]),
        pltpu.make_async_copy(cache_part(k_hbm, seq), token_rows(k_all, seq), load_sem.at[1]),
        pltpu.make_async_copy(cache_part(v_hbm, seq), token_rows(v_all, seq), load_sem.at[2]),
        pltpu.make_async_copy(proj_hbm, proj, load_sem.at[3]),
    ]
    loads = [
        pltpu.make_async_copy(wg_hbm, wg, load_sem.at[4]),
        pltpu.make_async_copy(wu_hbm, wu, load_sem.at[5]),
        pltpu.make_async_copy(wd_hbm, wd, load_sem.at[6]),
    ]
    for load in own_parts + loads:
        load.start()

    barrier = pltpu.get_barrier_semaphore()
    pl.semaphore_signal(barrier, 1, device_id=across, device_id_type=pl.DeviceIdType.MESH)
    pl.semaphore_signal(barrier, 1, device_id=partner, device_id_type=pl.DeviceIdType.MESH)

    pl.semaphore_signal(barrier, 1, device_id=diagonal, device_id_type=pl.DeviceIdType.MESH)

    @pl.when(has_high)
    def _():
        pl.semaphore_signal(barrier, 1, device_id=high, device_id_type=pl.DeviceIdType.MESH)

    @pl.when(has_low)
    def _():
        pl.semaphore_signal(barrier, 1, device_id=low, device_id_type=pl.DeviceIdType.MESH)

    peers = 3 + jnp.where(has_high, 1, 0) + jnp.where(has_low, 1, 0)
    pl.semaphore_wait(barrier, peers)

    others = (
        ((1 - y) * 2 + c, across),
        ((1 - y) * 2 + 1 - c, diagonal),
        (y * 2 + 1 - c, partner),
    )

    def scatter_copies(s, target):
        return (
            remote(
                cache_part(k_hbm, s),
                token_rows(k_all, seq),
                kv_send.at[s],
                kv_recv.at[seq],
                target,
            ),
            remote(
                cache_part(v_hbm, s),
                token_rows(v_all, seq),
                kv_send.at[4 + s],
                kv_recv.at[4 + seq],
                target,
            ),
            remote(
                query_part(s), token_rows(q_all, seq), q_send.at[s], q_recv.at[seq], target
            ),
        )

    for s, target in others:
        for copy in scatter_copies(s, target):
            copy.start()

    def arrival(ref, s, sem):
        return remote(token_rows(ref, s), token_rows(ref, s), q_send.at[s], sem, partner)

    for load in own_parts:
        load.wait()
    for s, _ in others:
        arrival(k_all, s, kv_recv.at[s]).wait_recv()
        arrival(v_all, s, kv_recv.at[4 + s]).wait_recv()
        arrival(q_all, s, q_recv.at[s]).wait_recv()

    far_copy = remote(
        token_rows(partial, (1 - y) * 2 + 1 - c), core_far, part_send.at[0], part_recv.at[0], partner
    )
    across_copy = remote(
        token_rows(partial, (1 - y) * 2 + c),
        across_near,
        part_send.at[1],
        part_recv.at[1],
        across,
    )
    near_copy = remote(
        token_rows(partial, y * 2 + 1 - c), core_near, part_send.at[2], part_recv.at[2], partner
    )

    def attend_step(j, carry):
        yy = jnp.where(j < 2, 1 - y, y)
        cc = jnp.where(j % 2 == 0, 1 - c, c)
        i = yy * 2 + cc
        at = pl.ds(pl.multiple_of(i * tokens, tokens), tokens)
        row_pos = i * tokens + lax.broadcasted_iota(jnp.int32, (tokens, length), 0)
        col_pos = lax.broadcasted_iota(jnp.int32, (tokens, length), 1)
        allowed = row_pos >= col_pos
        outputs = []
        for head in range(heads):
            scores = lax.dot_general(
                q_all[at, head * HD : (head + 1) * HD],
                k_all[...],
                (((1,), (1,)), ((), ())),
                preferred_element_type=jnp.float32,
            ) * (1.0 / HD**0.5)
            scores = jnp.where(allowed, scores, -1e30)
            weights = jnp.exp(scores - jnp.max(scores, axis=1, keepdims=True))
            total = jnp.sum(weights, axis=1, keepdims=True)
            probs = (weights * (1.0 / total)).astype(jnp.bfloat16)
            outputs.append(
                jnp.dot(probs, v_all[...], preferred_element_type=jnp.float32).astype(jnp.bfloat16)
            )
        projected = jnp.dot(
            jnp.concatenate(outputs, axis=1), proj[...], preferred_element_type=jnp.float32
        )

        @pl.when(j != 1)
        def _():
            partial[at, :] = projected.astype(jnp.bfloat16)

        @pl.when(j == 0)
        def _():
            far_copy.start()

        @pl.when(j == 1)
        def _():
            far_copy.wait_recv()
            partial[at, :] = (projected + core_far[...].astype(jnp.float32)).astype(jnp.bfloat16)
            across_copy.start()

        @pl.when(j == 2)
        def _():
            near_copy.start()

        return carry

    lax.fori_loop(0, 4, attend_step, 0)
    near_copy.wait_recv()
    own_rows = pl.ds(pl.multiple_of(seq * tokens, tokens), tokens)
    base = (
        residual_ref[...].astype(jnp.float32)
        + partial[own_rows, :].astype(jnp.float32)
        + core_near[...].astype(jnp.float32)
    )
    across_copy.wait_recv()
    hidden = (base + across_near[...].astype(jnp.float32)).astype(jnp.bfloat16)
    wide_ref[...] = hidden
    wide = hidden.astype(jnp.float32)
    normed = (
        wide
        * lax.rsqrt(jnp.mean(wide * wide, axis=1, keepdims=True) + 1e-06)
        * gain_ref[...].astype(jnp.float32)
    ).astype(jnp.bfloat16)
    own_slot = pl.ds(pl.multiple_of(slot(y, z, c) * tokens, tokens), tokens)
    rows[own_slot, :width] = normed
    rows[own_slot, width:] = coeff_ref[...]

    def row_copy(index, h, send, target):
        here = piece(rows, index, h)
        return remote(here, here, send, row_recv.at[index * 2 + h], target)

    def wait_rows(index, h):
        row_copy(index, h, relay_send.at[0], partner).wait_recv()

    def column_copies(p, h):
        index = slot(y, p, c)
        at = p * 2 + h
        return (
            (jnp.logical_and(p <= z, has_high), row_copy(index, h, up_send.at[at], high)),
            (jnp.logical_and(p >= z, has_low), row_copy(index, h, down_send.at[at], low)),
            (None, row_copy(index, h, y_send.at[at], across)),
            (None, row_copy(index, h, core_send.at[at], partner)),
        )

    def spread(p, h):
        for condition, copy in column_copies(p, h):
            if condition is None:
                copy.start()
            else:

                @pl.when(condition)
                def _():
                    copy.start()

    def relay_copy(p, h):
        return row_copy(slot(1 - y, p, c), h, relay_send.at[p * 2 + h], partner)

    def result_copy(yy, p):
        index = slot(yy, p, 1 - c)
        pair = yy * n_sub + p
        src = outs.at[pl.ds(pl.multiple_of(index * tokens, tokens), tokens), :]
        dst = from_core.at[pl.ds(pl.multiple_of(pair * tokens, tokens), tokens), :]
        return remote(src, dst, result_send.at[pair], core_recv.at[pair], partner)

    def compute(yy, p):
        wait_rows(slot(yy, p, 1 - c), 0)
        wait_rows(slot(yy, p, 1 - c), 1)
        at = pl.ds(pl.multiple_of((yy * n_sub + p) * 2 * tokens, 2 * tokens), 2 * tokens)
        x = rows[at, :width]
        gains = rows[at, width:].astype(jnp.float32)
        lane = lax.broadcasted_iota(jnp.int32, gains.shape, 1)
        coeff = jnp.sum(jnp.where(lane == me, gains, 0.0), axis=1, keepdims=True)
        gate = jnp.dot(x, wg[...], preferred_element_type=jnp.float32)
        up = jnp.dot(x, wu[...], preferred_element_type=jnp.float32)
        inner = (gate / (1.0 + jnp.exp(-gate)) * up).astype(jnp.bfloat16)
        out = jnp.dot(inner, wd[...], preferred_element_type=jnp.float32)
        outs[at, :] = (out * coeff).astype(jnp.bfloat16)
        result_copy(yy, p).start()

    for load in loads:
        load.wait()

    def gather_step(k, carry):
        t = (k + 1) // 2
        other = k % 2

        @pl.when(jnp.logical_or(k == 0, jnp.logical_and(other == 1, t < n_sub)))
        def _():
            p = lookup(order, z, t)

            @pl.when(t > 0)
            def _():
                wait_rows(slot(y, p, c), 0)

            spread(p, 0)

            @pl.when(t > 0)
            def _():
                wait_rows(slot(y, p, c), 1)

            spread(p, 1)

        @pl.when(other == 1)
        def _():
            p = lookup(order, z, t - 1)
            for h in range(2):
                wait_rows(slot(1 - y, p, c), h)
                relay_copy(p, h).start()

        compute(jnp.where(other == 1, 1 - y, y), lookup(order, z, t - other))
        return carry

    lax.fori_loop(0, 2 * n_sub, gather_step, 0)

    def wide_load(ref, index, h):
        at = pl.ds(pl.multiple_of(index * tokens + h * half, half), half)
        return ref[at, :].astype(jnp.float32)

    def y_copy(p, h):
        at = p * 2 + h
        return remote(
            piece(outs, slot(1 - y, p, c), h),
            piece(from_y, p, h),
            result_y_send.at[at],
            y_recv.at[at],
            across,
        )

    def z_copy(p, h, buffer, send, recv, target):
        at = p * 2 + h
        return remote(
            piece(outs, slot(y, p, c), h), piece(buffer, p, h), send.at[at], recv.at[at], target
        )

    def up_copy(p, h):
        return z_copy(p, h, from_low, result_up_send, low_recv, high)

    def down_copy(p, h):
        return z_copy(p, h, from_high, result_down_send, high_recv, low)

    def store_out(index, h, value):
        at = pl.ds(pl.multiple_of(index * tokens + h * half, half), half)
        outs[at, :] = value.astype(jnp.bfloat16)

    def y_step(k, carry):
        p = lookup(order, z, n_sub - 1 - k)
        result_copy(1 - y, p).wait_recv()
        index = slot(1 - y, p, c)
        for h in range(2):
            store_out(
                index, h, wide_load(outs, index, h) + wide_load(from_core, (1 - y) * n_sub + p, h)
            )
            y_copy(p, h).start()
        return carry

    lax.fori_loop(0, n_sub, y_step, 0)

    def own_step(k, carry):
        p = lookup(order, z, n_sub - 1 - k)
        result_copy(y, p).wait_recv()
        index = slot(y, p, c)
        store = wide_load(outs, index, 0) + wide_load(from_core, y * n_sub + p, 0)
        store_out(index, 0, store)
        store = wide_load(outs, index, 1) + wide_load(from_core, y * n_sub + p, 1)
        store_out(index, 1, store)
        return carry

    lax.fori_loop(0, n_sub, own_step, 0)

    def z_step(k, carry):
        p = lookup(order, z, n_sub - 1 - k // 2)
        h = k % 2
        index = slot(y, p, c)
        y_copy(p, h).wait_recv()

        @pl.when(p > z)
        def _():
            store_out(index, h, wide_load(outs, index, h) + wide_load(from_y, p, h))

            @pl.when(has_low)
            def _():
                up_copy(p, h).wait_recv()
                store_out(index, h, wide_load(outs, index, h) + wide_load(from_low, p, h))

            up_copy(p, h).start()

        @pl.when(p < z)
        def _():
            store_out(index, h, wide_load(outs, index, h) + wide_load(from_y, p, h))

            @pl.when(has_high)
            def _():
                down_copy(p, h).wait_recv()
                store_out(index, h, wide_load(outs, index, h) + wide_load(from_high, p, h))

            down_copy(p, h).start()

        @pl.when(p == z)
        def _():
            at = pl.ds(pl.multiple_of(h * half, half), half)
            store_out(index, h, wide_load(outs, index, h) + wide_load(from_y, p, h))

            @pl.when(has_low)
            def _():
                up_copy(p, h).wait_recv()
                store_out(index, h, wide_load(outs, index, h) + wide_load(from_low, p, h))

            @pl.when(has_high)
            def _():
                down_copy(p, h).wait_recv()
                store_out(index, h, wide_load(outs, index, h) + wide_load(from_high, p, h))

            o_ref[at, :] = (wide_ref[at, :].astype(jnp.float32) + wide_load(outs, index, h)).astype(
                jnp.bfloat16
            )

        return carry

    lax.fori_loop(0, 2 * n_sub, z_step, 0)

    def drain(k, carry):
        p = k // 2
        h = k % 2
        for condition, copy in column_copies(p, h):
            if condition is None:
                copy.wait_send()
            else:

                @pl.when(condition)
                def _():
                    copy.wait_send()

        relay_copy(p, h).wait_send()
        y_copy(p, h).wait_send()
        result_copy(h, p).wait_send()

        @pl.when(p > z)
        def _():
            up_copy(p, h).wait_send()

        @pl.when(p < z)
        def _():
            down_copy(p, h).wait_send()

        return carry

    lax.fori_loop(0, 2 * n_sub, drain, 0)
    for s, target in others:
        for copy in scatter_copies(s, target):
            copy.wait_send()
    far_copy.wait_send()
    across_copy.wait_send()
    near_copy.wait_send()


def layer(queries, keys, values, residual, proj, gain, coeffs, w_gate, w_up, w_down, n_sub):
    tokens, width = residual.shape
    share = proj.shape[0]
    blocks = 4 * n_sub
    dma = lambda count: pltpu.SemaphoreType.DMA((count,))
    hbm = pl.BlockSpec(memory_space=pl.ANY)
    vmem = pl.BlockSpec(memory_space=pltpu.VMEM)
    bf = jnp.bfloat16
    return pl.pallas_call(
        functools.partial(layer_kernel, n_sub),
        in_specs=[hbm, hbm, hbm, vmem, hbm, vmem, vmem, hbm, hbm, hbm],
        out_specs=vmem,
        out_shape=jax.ShapeDtypeStruct((tokens, width), bf),
        scratch_shapes=[
            pltpu.VMEM((4 * tokens, share), bf),
            pltpu.VMEM((4 * tokens, HD), bf),
            pltpu.VMEM((4 * tokens, HD), bf),
            pltpu.VMEM(proj.shape, bf),
            pltpu.VMEM((4 * tokens, width), bf),
            pltpu.VMEM((tokens, width), bf),
            pltpu.VMEM((tokens, width), bf),
            pltpu.VMEM((tokens, width), bf),
            pltpu.VMEM((tokens, width), bf),
            dma(4),
            dma(4),
            dma(8),
            dma(8),
            dma(3),
            dma(3),
            pltpu.VMEM((blocks * tokens, width + coeffs.shape[1]), bf),
            pltpu.VMEM((blocks * tokens, width), bf),
            pltpu.VMEM((2 * n_sub * tokens, width), bf),
            pltpu.VMEM((n_sub * tokens, width), bf),
            pltpu.VMEM((n_sub * tokens, width), bf),
            pltpu.VMEM((n_sub * tokens, width), bf),
            pltpu.VMEM(w_gate.shape, bf),
            pltpu.VMEM(w_up.shape, bf),
            pltpu.VMEM(w_down.shape, bf),
            dma(7),
            dma(2 * blocks),
            dma(2 * n_sub),
            dma(2 * n_sub),
            dma(2 * n_sub),
            dma(2 * n_sub),
            dma(2 * n_sub),
            dma(2 * n_sub),
            dma(2 * n_sub),
            dma(2 * n_sub),
            dma(2 * n_sub),
            dma(2 * n_sub),
            dma(2 * n_sub),
            dma(2 * n_sub),
            dma(2 * n_sub),
        ],
        compiler_params=pltpu.CompilerParams(
            collective_id=0, has_side_effects=True, vmem_limit_bytes=60 * 2**20
        ),
        name="layer",
    )(queries, keys, values, residual, proj, gain, coeffs, w_gate, w_up, w_down)


def per_device_dense(
    query_rows,
    key_rows,
    value_rows,
    residual_in,
    out_proj,
    norm_gain,
    expert_ids,
    gate_weights,
    expert_gate,
    expert_up,
    expert_down,
):
    n_seq = lax.axis_size("seq")
    n_sub = lax.axis_size("sub")
    experts = n_seq * n_sub
    chosen = expert_ids[0][:, :, None] == jnp.arange(experts, dtype=jnp.int32)[None, None, :]
    coeffs_local = jnp.sum(
        jnp.where(chosen, gate_weights[0].astype(jnp.float32)[:, :, None], 0.0), axis=1
    ).astype(jnp.bfloat16)

    lanes = 128 * ((experts + 127) // 128)
    coeffs = jnp.pad(coeffs_local, ((0, 0), (0, lanes - experts)))
    return layer(
        query_rows[0],
        key_rows[0],
        value_rows[0],
        residual_in[0],
        out_proj,
        norm_gain[None],
        coeffs,
        expert_gate[0],
        expert_up[0],
        expert_down[0],
        n_sub,
    )[None]


def per_device(*args):
    tokens = args[0].shape[1]
    topk = args[6].shape[2]
    n_seq = lax.axis_size("seq")
    experts = n_seq * lax.axis_size("sub")
    cap = max(2, (5 * tokens * topk + 4 * experts - 1) // (4 * experts))
    if 2 * cap >= tokens and n_seq == 4:
        return per_device_dense(*args)
    return per_device_routed(*args)


def solution(mesh):
    placed = (
        P(("grp", "sub"), "seq", None),
        P(("grp", "sub"), "seq", None),
        P(("grp", "sub"), "seq", None),
        P(("grp", "sub"), "seq", None),
        P("seq", None),
        P(),
        P(("grp", "sub"), "seq", None),
        P(("grp", "sub"), "seq", None),
        P(("seq", "sub"), None, None),
        P(("seq", "sub"), None, None),
        P(("seq", "sub"), None, None),
    )
    return jax.shard_map(
        per_device,
        mesh=mesh,
        in_specs=placed,
        out_specs=P(("grp", "sub"), "seq", None),
        check_vma=False,
    )
```

```python
import functools
import jax
import jax.numpy as jnp
from jax import lax
from jax.experimental import pallas as pl
from jax.experimental.pallas import tpu as pltpu
from jax.sharding import PartitionSpec as P

D = 2048
HD = 128
QH = 16
KVH = 2


def attend_head(queries, keys_one, values_one, block):
    length = queries.shape[0]
    scale = 1.0 / queries.shape[1] ** 0.5
    pieces = []
    for part_index in range(length // block):
        stop = (part_index + 1) * block
        rows_here = queries[part_index * block : stop]
        scores = (
            jnp.einsum("qd,kd->qk", rows_here, keys_one[:stop], preferred_element_type=jnp.float32)
            * scale
        )
        row_pos = part_index * block + jnp.arange(block, dtype=jnp.int32)
        col_pos = jnp.arange(stop, dtype=jnp.int32)
        scores = jnp.where(row_pos[:, None] >= col_pos[None, :], scores, -1e30)
        peak = jnp.max(scores, axis=1, keepdims=True)
        weights = jnp.exp(scores - peak)
        probs = (weights / jnp.sum(weights, axis=1, keepdims=True)).astype(jnp.bfloat16)
        pieces.append(
            jnp.dot(probs, values_one[:stop], preferred_element_type=jnp.float32).astype(
                jnp.bfloat16
            )
        )
    return jnp.concatenate(pieces, axis=0)


def rank_in_expert(flat_ids, experts):
    items = flat_ids.shape[0]
    width = 128
    n_parts = items // width
    onehot = (
        (flat_ids[:, None] == jnp.arange(experts, dtype=jnp.int32)[None, :])
        .astype(jnp.bfloat16)
        .reshape(n_parts, width, experts)
    )
    lower = (
        jnp.arange(width, dtype=jnp.int32)[:, None] > jnp.arange(width, dtype=jnp.int32)[None, :]
    ).astype(jnp.bfloat16)
    within = jnp.einsum("ij,bje->bie", lower, onehot, preferred_element_type=jnp.float32)
    part_counts = jnp.sum(onehot.astype(jnp.float32), axis=1)
    earlier = jnp.cumsum(part_counts, axis=0) - part_counts
    ranks = jnp.sum((within + earlier[:, None, :]) * onehot.astype(jnp.float32), axis=2)
    return ranks.reshape(items).astype(jnp.int32)


def per_device_routed(
    query_rows,
    key_rows,
    value_rows,
    residual_in,
    out_proj,
    norm_gain,
    expert_ids,
    gate_weights,
    expert_gate,
    expert_up,
    expert_down,
):
    tokens = query_rows.shape[1]
    n_seq = lax.axis_size("seq")
    n_sub = lax.axis_size("sub")
    heads_here = QH // n_seq
    group = QH // KVH
    query_local = lax.all_to_all(query_rows, "seq", split_axis=2, concat_axis=1, tiled=True)
    key_full, value_full = (
        lax.all_gather(key_rows, "seq", axis=1, tiled=True),
        lax.all_gather(value_rows, "seq", axis=1, tiled=True),
    )
    first_head = lax.axis_index("seq") * heads_here
    key_list = []
    value_list = []
    for head in range(heads_here):
        kv_start = (first_head + head) // group * HD
        key_list.append(lax.dynamic_slice_in_dim(key_full[0], kv_start, HD, 1))
        value_list.append(lax.dynamic_slice_in_dim(value_full[0], kv_start, HD, 1))
    length = query_local.shape[1]
    block = min(length, max(512, length // 8))
    outputs = [
        attend_head(
            query_local[0, :, head * HD : (head + 1) * HD], key_list[head], value_list[head], block
        )
        for head in range(heads_here)
    ]
    head_block = jnp.concatenate(outputs, axis=1)[None]
    attended = lax.all_to_all(head_block, "seq", split_axis=1, concat_axis=2, tiled=True)[0]
    projected = jnp.dot(
        attended,
        lax.all_gather(out_proj, "seq", axis=0, tiled=True),
        preferred_element_type=jnp.float32,
    )
    hidden = (residual_in[0].astype(jnp.float32) + projected).astype(jnp.bfloat16)
    wide = hidden.astype(jnp.float32)
    normed = (
        wide
        * lax.rsqrt(jnp.mean(wide * wide, axis=1, keepdims=True) + 1e-06)
        * norm_gain.astype(jnp.float32)
    ).astype(jnp.bfloat16)
    topk = expert_ids.shape[2]
    experts = n_seq * n_sub
    cap = max(2, (5 * tokens * topk + 4 * experts - 1) // (4 * experts))
    flat_ids = expert_ids[0].reshape(-1)
    items = flat_ids.shape[0]
    ranks = rank_in_expert(flat_ids, experts)
    slot_of = flat_ids * cap + ranks
    slots_out = experts * cap
    item_of_slot = (
        jnp.full((slots_out,), items, jnp.int32).at[slot_of].set(jnp.arange(items, dtype=jnp.int32))
    )
    padded_rows = jnp.concatenate([normed, jnp.zeros((1, D), jnp.bfloat16)], axis=0)
    padded_gates = jnp.concatenate(
        [gate_weights[0].reshape(-1), jnp.zeros((1,), jnp.bfloat16)], axis=0
    )
    token_of_slot = jnp.where(item_of_slot < items, item_of_slot // topk, tokens)
    send_rows = padded_rows[token_of_slot].reshape(experts, cap, D)
    send_gates = padded_gates[item_of_slot].reshape(experts, cap)
    recv_rows, recv_gates = (
        lax.all_to_all(send_rows, ("seq", "sub"), split_axis=0, concat_axis=0, tiled=True),
        lax.all_to_all(send_gates, ("seq", "sub"), split_axis=0, concat_axis=0, tiled=True),
    )
    slots_in = experts * cap
    valid = recv_gates > 0
    counts = jnp.sum(valid.astype(jnp.int32), axis=1)
    offsets = jnp.cumsum(counts) - counts
    dest = jnp.where(
        valid, offsets[:, None] + jnp.arange(cap, dtype=jnp.int32)[None, :], slots_in
    ).reshape(-1)
    source_of = (
        jnp.full((slots_in + 1,), slots_in, jnp.int32)
        .at[dest]
        .set(jnp.arange(slots_in, dtype=jnp.int32))[:slots_in]
    )
    compact_rows = jnp.concatenate(
        [recv_rows.reshape(slots_in, D), jnp.zeros((1, D), jnp.bfloat16)], axis=0
    )[source_of]
    compact_gates = jnp.concatenate(
        [recv_gates.reshape(-1), jnp.zeros((1,), jnp.bfloat16)], axis=0
    )[source_of].astype(jnp.float32)
    filled = jnp.sum(counts)
    n_blocks = (filled + slots_in - 1) // slots_in
    w_gate = expert_gate[0]
    w_up = expert_up[0]
    w_down = expert_down[0]

    def expert_block(index, results):
        gate_proj = jnp.dot(compact_rows, w_gate, preferred_element_type=jnp.float32)
        up_proj = jnp.dot(compact_rows, w_up, preferred_element_type=jnp.float32)
        inner = (jax.nn.silu(gate_proj) * up_proj).astype(jnp.bfloat16)
        weighted = (
            jnp.dot(inner, w_down, preferred_element_type=jnp.float32) * compact_gates[:, None]
        )
        return weighted.astype(jnp.bfloat16)

    results = lax.fori_loop(0, n_blocks, expert_block, jnp.zeros((slots_in, D), jnp.bfloat16))
    returned = jnp.concatenate([results, jnp.zeros((1, D), jnp.bfloat16)], axis=0)[dest].reshape(
        experts, cap, D
    )
    back = lax.all_to_all(
        returned, ("seq", "sub"), split_axis=0, concat_axis=0, tiled=True
    ).reshape(slots_out, D)
    gathered = back[slot_of].reshape(tokens, topk, D).astype(jnp.float32)
    mixture = jnp.sum(gathered, axis=1)
    return (wide + mixture).astype(jnp.bfloat16)[None]


def nearest_order(n):
    return [sorted(range(n), key=lambda p: (abs(p - z), p)) for z in range(n)]


def lookup(table, i, j):
    total = 0
    for a, row in enumerate(table):
        for b, value in enumerate(row):
            if value:
                hit = jnp.logical_and(i == a, j == b)
                total = total + jnp.where(hit, value, 0)
    return total


def layer_kernel(
    n_sub,
    q_hbm,
    k_hbm,
    v_hbm,
    residual_ref,
    proj_hbm,
    gain_ref,
    coeff_ref,
    wg_hbm,
    wu_hbm,
    wd_hbm,
    o_ref,
    q_all,
    k_all,
    v_all,
    proj,
    partial,
    core_far,
    core_near,
    across_near,
    wide_ref,
    q_send,
    q_recv,
    kv_send,
    kv_recv,
    part_send,
    part_recv,
    rows,
    outs,
    from_core,
    from_y,
    from_low,
    from_high,
    from_mate,
    wg,
    wu,
    wd,
    load_sem,
    row_recv,
    up_send,
    down_send,
    y_send,
    core_send,
    relay_send,
    core_recv,
    result_send,
    y_recv,
    result_y_send,
    low_recv,
    high_recv,
    result_up_send,
    result_down_send,
    mate_send,
    mate_recv,
):
    seq = lax.axis_index("seq")
    z = lax.axis_index("sub")
    y = seq // 2
    c = seq % 2
    tokens = residual_ref.shape[0]
    width = residual_ref.shape[1]
    share = q_all.shape[1]
    heads = share // HD
    length = q_all.shape[0]
    group = QH // KVH
    half = tokens // 2
    order = nearest_order(n_sub)
    me = seq * n_sub + z
    high = {"sub": z + 1}
    low = {"sub": z - 1}
    across = {"seq": (1 - y) * 2 + c}
    partner = {"seq": y * 2 + 1 - c}
    diagonal = {"seq": (1 - y) * 2 + 1 - c}
    mate = z + 1 - 2 * (z % 2)
    beside = {"sub": mate}
    has_high = z < n_sub - 1
    has_low = z > 0

    def slot(yy, p, cc):
        return (yy * n_sub + p) * 2 + cc

    def piece(ref, index, h):
        return ref.at[pl.ds(pl.multiple_of(index * tokens + h * half, half), half), :]

    def remote(src, dst, send, recv, target):
        return pltpu.make_async_remote_copy(
            src_ref=src,
            dst_ref=dst,
            send_sem=send,
            recv_sem=recv,
            device_id=target,
            device_id_type=pl.DeviceIdType.MESH,
        )

    def query_part(s):
        return q_hbm.at[:, pl.ds(pl.multiple_of(s * share, share), share)]

    def cache_part(ref, s):
        return ref.at[:, pl.ds(pl.multiple_of(s * heads // group * HD, HD), HD)]

    def token_rows(ref, s):
        return ref.at[pl.ds(pl.multiple_of(s * tokens, tokens), tokens), :]

    own_parts = [
        pltpu.make_async_copy(query_part(seq), token_rows(q_all, seq), load_sem.at[0]),
        pltpu.make_async_copy(cache_part(k_hbm, seq), token_rows(k_all, seq), load_sem.at[1]),
        pltpu.make_async_copy(cache_part(v_hbm, seq), token_rows(v_all, seq), load_sem.at[2]),
        pltpu.make_async_copy(proj_hbm, proj, load_sem.at[3]),
    ]
    loads = [
        pltpu.make_async_copy(wg_hbm, wg, load_sem.at[4]),
        pltpu.make_async_copy(wu_hbm, wu, load_sem.at[5]),
        pltpu.make_async_copy(wd_hbm, wd, load_sem.at[6]),
    ]
    for load in own_parts + loads:
        load.start()

    barrier = pltpu.get_barrier_semaphore()
    pl.semaphore_signal(barrier, 1, device_id=across, device_id_type=pl.DeviceIdType.MESH)
    pl.semaphore_signal(barrier, 1, device_id=partner, device_id_type=pl.DeviceIdType.MESH)

    pl.semaphore_signal(barrier, 1, device_id=diagonal, device_id_type=pl.DeviceIdType.MESH)

    @pl.when(has_high)
    def _():
        pl.semaphore_signal(barrier, 1, device_id=high, device_id_type=pl.DeviceIdType.MESH)

    @pl.when(has_low)
    def _():
        pl.semaphore_signal(barrier, 1, device_id=low, device_id_type=pl.DeviceIdType.MESH)

    peers = 3 + jnp.where(has_high, 1, 0) + jnp.where(has_low, 1, 0)
    pl.semaphore_wait(barrier, peers)

    others = (
        ((1 - y) * 2 + c, across),
        ((1 - y) * 2 + 1 - c, diagonal),
        (y * 2 + 1 - c, partner),
    )

    def scatter_copies(s, target):
        return (
            remote(
                cache_part(k_hbm, s),
                token_rows(k_all, seq),
                kv_send.at[s],
                kv_recv.at[seq],
                target,
            ),
            remote(
                cache_part(v_hbm, s),
                token_rows(v_all, seq),
                kv_send.at[4 + s],
                kv_recv.at[4 + seq],
                target,
            ),
            remote(
                query_part(s), token_rows(q_all, seq), q_send.at[s], q_recv.at[seq], target
            ),
        )

    for s, target in others:
        for copy in scatter_copies(s, target):
            copy.start()

    def arrival(ref, s, sem):
        return remote(token_rows(ref, s), token_rows(ref, s), q_send.at[s], sem, partner)

    for load in own_parts:
        load.wait()
    for s, _ in others:
        arrival(k_all, s, kv_recv.at[s]).wait_recv()
        arrival(v_all, s, kv_recv.at[4 + s]).wait_recv()
        arrival(q_all, s, q_recv.at[s]).wait_recv()

    far_copy = remote(
        token_rows(partial, (1 - y) * 2 + 1 - c), core_far, part_send.at[0], part_recv.at[0], partner
    )
    across_copy = remote(
        token_rows(partial, (1 - y) * 2 + c),
        across_near,
        part_send.at[1],
        part_recv.at[1],
        across,
    )
    near_copy = remote(
        token_rows(partial, y * 2 + 1 - c), core_near, part_send.at[2], part_recv.at[2], partner
    )

    def attend_step(j, carry):
        yy = jnp.where(j < 2, 1 - y, y)
        cc = jnp.where(j % 2 == 0, 1 - c, c)
        i = yy * 2 + cc
        at = pl.ds(pl.multiple_of(i * tokens, tokens), tokens)
        row_pos = i * tokens + lax.broadcasted_iota(jnp.int32, (tokens, length), 0)
        col_pos = lax.broadcasted_iota(jnp.int32, (tokens, length), 1)
        allowed = row_pos >= col_pos
        outputs = []
        for head in range(heads):
            scores = lax.dot_general(
                q_all[at, head * HD : (head + 1) * HD],
                k_all[...],
                (((1,), (1,)), ((), ())),
                preferred_element_type=jnp.float32,
            ) * (1.0 / HD**0.5)
            scores = jnp.where(allowed, scores, -1e30)
            weights = jnp.exp(scores - jnp.max(scores, axis=1, keepdims=True))
            total = jnp.sum(weights, axis=1, keepdims=True)
            probs = (weights * (1.0 / total)).astype(jnp.bfloat16)
            outputs.append(
                jnp.dot(probs, v_all[...], preferred_element_type=jnp.float32).astype(jnp.bfloat16)
            )
        projected = jnp.dot(
            jnp.concatenate(outputs, axis=1), proj[...], preferred_element_type=jnp.float32
        )

        @pl.when(j != 1)
        def _():
            partial[at, :] = projected.astype(jnp.bfloat16)

        @pl.when(j == 0)
        def _():
            far_copy.start()

        @pl.when(j == 1)
        def _():
            far_copy.wait_recv()
            partial[at, :] = (projected + core_far[...].astype(jnp.float32)).astype(jnp.bfloat16)
            across_copy.start()

        @pl.when(j == 2)
        def _():
            near_copy.start()

        return carry

    lax.fori_loop(0, 4, attend_step, 0)
    near_copy.wait_recv()
    own_rows = pl.ds(pl.multiple_of(seq * tokens, tokens), tokens)
    base = (
        residual_ref[...].astype(jnp.float32)
        + partial[own_rows, :].astype(jnp.float32)
        + core_near[...].astype(jnp.float32)
    )
    across_copy.wait_recv()
    hidden = (base + across_near[...].astype(jnp.float32)).astype(jnp.bfloat16)
    wide_ref[...] = hidden
    wide = hidden.astype(jnp.float32)
    normed = (
        wide
        * lax.rsqrt(jnp.mean(wide * wide, axis=1, keepdims=True) + 1e-06)
        * gain_ref[...].astype(jnp.float32)
    ).astype(jnp.bfloat16)
    own_slot = pl.ds(pl.multiple_of(slot(y, z, c) * tokens, tokens), tokens)
    rows[own_slot, :width] = normed
    rows[own_slot, width:] = coeff_ref[...]

    def row_copy(index, h, send, target):
        here = piece(rows, index, h)
        return remote(here, here, send, row_recv.at[index * 2 + h], target)

    def wait_rows(index, h):
        row_copy(index, h, relay_send.at[0], partner).wait_recv()

    def column_copies(p, h):
        index = slot(y, p, c)
        at = p * 2 + h
        return (
            (jnp.logical_and(p <= z, has_high), row_copy(index, h, up_send.at[at], high)),
            (jnp.logical_and(p >= z, has_low), row_copy(index, h, down_send.at[at], low)),
            (
                jnp.logical_or(p != mate, h == 0),
                row_copy(index, h, y_send.at[at], across),
            ),
            (None, row_copy(index, h, core_send.at[at], partner)),
        )

    def spread(p, h):
        for condition, copy in column_copies(p, h):
            if condition is None:
                copy.start()
            else:

                @pl.when(condition)
                def _():
                    copy.start()

    def relay_copy(p, h):
        return row_copy(slot(1 - y, p, c), h, relay_send.at[p * 2 + h], partner)

    def result_copy(yy, p):
        index = slot(yy, p, 1 - c)
        pair = yy * n_sub + p
        src = outs.at[pl.ds(pl.multiple_of(index * tokens, tokens), tokens), :]
        dst = from_core.at[pl.ds(pl.multiple_of(pair * tokens, tokens), tokens), :]
        return remote(src, dst, result_send.at[pair], core_recv.at[pair], partner)

    def compute(yy, p):
        wait_rows(slot(yy, p, 1 - c), 0)
        wait_rows(slot(yy, p, 1 - c), 1)
        at = pl.ds(pl.multiple_of((yy * n_sub + p) * 2 * tokens, 2 * tokens), 2 * tokens)
        x = rows[at, :width]
        gains = rows[at, width:].astype(jnp.float32)
        lane = lax.broadcasted_iota(jnp.int32, gains.shape, 1)
        coeff = jnp.sum(jnp.where(lane == me, gains, 0.0), axis=1, keepdims=True)
        gate = jnp.dot(x, wg[...], preferred_element_type=jnp.float32)
        up = jnp.dot(x, wu[...], preferred_element_type=jnp.float32)
        inner = (gate / (1.0 + jnp.exp(-gate)) * up).astype(jnp.bfloat16)
        out = jnp.dot(inner, wd[...], preferred_element_type=jnp.float32)
        outs[at, :] = (out * coeff).astype(jnp.bfloat16)
        result_copy(yy, p).start()

    for load in loads:
        load.wait()

    def mate_rows():
        return row_copy(slot(1 - y, z, c), 1, mate_send.at[0], beside)

    def gather_step(k, carry):
        t = (k + 1) // 2
        other = k % 2
        last = k == 2 * n_sub

        @pl.when(jnp.logical_or(k == 0, jnp.logical_and(other == 1, t < n_sub)))
        def _():
            p = lookup(order, z, t)

            @pl.when(t > 0)
            def _():
                wait_rows(slot(y, p, c), 0)

            spread(p, 0)

            @pl.when(t > 0)
            def _():
                wait_rows(slot(y, p, c), 1)

            spread(p, 1)

        @pl.when(k == 2 * n_sub - 3)
        def _():
            mate_rows().start()

        q = lookup(order, z, t - 1)

        @pl.when(other == 1)
        def _():
            wait_rows(slot(1 - y, q, c), 0)
            relay_copy(q, 0).start()

            @pl.when(q != mate)
            def _():
                wait_rows(slot(1 - y, q, c), 1)
                relay_copy(q, 1).start()

        @pl.when(last)
        def _():
            wait_rows(slot(1 - y, mate, c), 1)
            relay_copy(mate, 1).start()

        @pl.when(jnp.logical_or(other == 0, q != mate))
        def _():
            yy = jnp.where(jnp.logical_or(other == 1, last), 1 - y, y)
            p = jnp.where(last, mate, jnp.where(other == 1, q, lookup(order, z, t)))
            compute(yy, p)

        return carry

    lax.fori_loop(0, 2 * n_sub + 1, gather_step, 0)

    def wide_load(ref, index, h):
        at = pl.ds(pl.multiple_of(index * tokens + h * half, half), half)
        return ref[at, :].astype(jnp.float32)

    def y_copy(p, h):
        at = p * 2 + h
        return remote(
            piece(outs, slot(1 - y, p, c), h),
            piece(from_y, p, h),
            result_y_send.at[at],
            y_recv.at[at],
            across,
        )

    def z_copy(p, h, buffer, send, recv, target):
        at = p * 2 + h
        return remote(
            piece(outs, slot(y, p, c), h), piece(buffer, p, h), send.at[at], recv.at[at], target
        )

    def up_copy(p, h):
        return z_copy(p, h, from_low, result_up_send, low_recv, high)

    def down_copy(p, h):
        return z_copy(p, h, from_high, result_down_send, high_recv, low)

    def store_out(index, h, value):
        at = pl.ds(pl.multiple_of(index * tokens + h * half, half), half)
        outs[at, :] = value.astype(jnp.bfloat16)

    def mate_result(p):
        return remote(
            piece(outs, slot(1 - y, p, c), 1), from_mate, mate_send.at[1], mate_recv.at[0], beside
        )

    def y_step(k, carry):
        p = lookup(order, z, n_sub - 1 - k)
        result_copy(1 - y, p).wait_recv()
        index = slot(1 - y, p, c)
        for h in range(2):
            store_out(
                index, h, wide_load(outs, index, h) + wide_load(from_core, (1 - y) * n_sub + p, h)
            )

            @pl.when(jnp.logical_and(p == mate, h == 1))
            def _():
                mate_result(mate).start()

            @pl.when(jnp.logical_or(p != z, h == 0) & jnp.logical_or(p != mate, h == 0))
            def _():
                y_copy(p, h).start()

        return carry

    lax.fori_loop(0, n_sub, y_step, 0)

    def own_step(k, carry):
        p = lookup(order, z, n_sub - 1 - k)
        result_copy(y, p).wait_recv()
        index = slot(y, p, c)
        store = wide_load(outs, index, 0) + wide_load(from_core, y * n_sub + p, 0)
        store_out(index, 0, store)
        store = wide_load(outs, index, 1) + wide_load(from_core, y * n_sub + p, 1)
        store_out(index, 1, store)
        return carry

    lax.fori_loop(0, n_sub, own_step, 0)
    mate_result(z).wait_recv()
    store_out(
        slot(1 - y, z, c),
        1,
        wide_load(outs, slot(1 - y, z, c), 1) + from_mate[...].astype(jnp.float32),
    )
    y_copy(z, 1).start()

    def z_step(k, carry):
        p = lookup(order, z, n_sub - 1 - k // 2)
        h = k % 2
        index = slot(y, p, c)
        direct = jnp.logical_or(p != mate, h == 0)

        @pl.when(direct)
        def _():
            y_copy(p, h).wait_recv()
            store_out(index, h, wide_load(outs, index, h) + wide_load(from_y, p, h))

        @pl.when(p > z)
        def _():
            @pl.when(has_low)
            def _():
                up_copy(p, h).wait_recv()
                store_out(index, h, wide_load(outs, index, h) + wide_load(from_low, p, h))

            up_copy(p, h).start()

        @pl.when(p < z)
        def _():
            @pl.when(has_high)
            def _():
                down_copy(p, h).wait_recv()
                store_out(index, h, wide_load(outs, index, h) + wide_load(from_high, p, h))

            down_copy(p, h).start()

        @pl.when(p == z)
        def _():
            at = pl.ds(pl.multiple_of(h * half, half), half)
            @pl.when(has_low)
            def _():
                up_copy(p, h).wait_recv()
                store_out(index, h, wide_load(outs, index, h) + wide_load(from_low, p, h))

            @pl.when(has_high)
            def _():
                down_copy(p, h).wait_recv()
                store_out(index, h, wide_load(outs, index, h) + wide_load(from_high, p, h))

            o_ref[at, :] = (wide_ref[at, :].astype(jnp.float32) + wide_load(outs, index, h)).astype(
                jnp.bfloat16
            )

        return carry

    lax.fori_loop(0, 2 * n_sub, z_step, 0)

    def drain(k, carry):
        p = k // 2
        h = k % 2
        for condition, copy in column_copies(p, h):
            if condition is None:
                copy.wait_send()
            else:

                @pl.when(condition)
                def _():
                    copy.wait_send()

        relay_copy(p, h).wait_send()

        @pl.when(jnp.logical_or(p != mate, h == 0))
        def _():
            y_copy(p, h).wait_send()

        result_copy(h, p).wait_send()

        @pl.when(p > z)
        def _():
            up_copy(p, h).wait_send()

        @pl.when(p < z)
        def _():
            down_copy(p, h).wait_send()

        return carry

    lax.fori_loop(0, 2 * n_sub, drain, 0)
    for s, target in others:
        for copy in scatter_copies(s, target):
            copy.wait_send()
    mate_rows().wait_send()
    mate_result(mate).wait_send()
    far_copy.wait_send()
    across_copy.wait_send()
    near_copy.wait_send()


def layer(queries, keys, values, residual, proj, gain, coeffs, w_gate, w_up, w_down, n_sub):
    tokens, width = residual.shape
    share = proj.shape[0]
    blocks = 4 * n_sub
    dma = lambda count: pltpu.SemaphoreType.DMA((count,))
    hbm = pl.BlockSpec(memory_space=pl.ANY)
    vmem = pl.BlockSpec(memory_space=pltpu.VMEM)
    bf = jnp.bfloat16
    return pl.pallas_call(
        functools.partial(layer_kernel, n_sub),
        in_specs=[hbm, hbm, hbm, vmem, hbm, vmem, vmem, hbm, hbm, hbm],
        out_specs=vmem,
        out_shape=jax.ShapeDtypeStruct((tokens, width), bf),
        scratch_shapes=[
            pltpu.VMEM((4 * tokens, share), bf),
            pltpu.VMEM((4 * tokens, HD), bf),
            pltpu.VMEM((4 * tokens, HD), bf),
            pltpu.VMEM(proj.shape, bf),
            pltpu.VMEM((4 * tokens, width), bf),
            pltpu.VMEM((tokens, width), bf),
            pltpu.VMEM((tokens, width), bf),
            pltpu.VMEM((tokens, width), bf),
            pltpu.VMEM((tokens, width), bf),
            dma(4),
            dma(4),
            dma(8),
            dma(8),
            dma(3),
            dma(3),
            pltpu.VMEM((blocks * tokens, width + coeffs.shape[1]), bf),
            pltpu.VMEM((blocks * tokens, width), bf),
            pltpu.VMEM((2 * n_sub * tokens, width), bf),
            pltpu.VMEM((n_sub * tokens, width), bf),
            pltpu.VMEM((n_sub * tokens, width), bf),
            pltpu.VMEM((n_sub * tokens, width), bf),
            pltpu.VMEM((tokens // 2, width), bf),
            pltpu.VMEM(w_gate.shape, bf),
            pltpu.VMEM(w_up.shape, bf),
            pltpu.VMEM(w_down.shape, bf),
            dma(7),
            dma(2 * blocks),
            dma(2 * n_sub),
            dma(2 * n_sub),
            dma(2 * n_sub),
            dma(2 * n_sub),
            dma(2 * n_sub),
            dma(2 * n_sub),
            dma(2 * n_sub),
            dma(2 * n_sub),
            dma(2 * n_sub),
            dma(2 * n_sub),
            dma(2 * n_sub),
            dma(2 * n_sub),
            dma(2 * n_sub),
            dma(2),
            dma(1),
        ],
        compiler_params=pltpu.CompilerParams(
            collective_id=0, has_side_effects=True, vmem_limit_bytes=60 * 2**20
        ),
        name="layer",
    )(queries, keys, values, residual, proj, gain, coeffs, w_gate, w_up, w_down)


def per_device_dense(
    query_rows,
    key_rows,
    value_rows,
    residual_in,
    out_proj,
    norm_gain,
    expert_ids,
    gate_weights,
    expert_gate,
    expert_up,
    expert_down,
):
    n_seq = lax.axis_size("seq")
    n_sub = lax.axis_size("sub")
    experts = n_seq * n_sub
    chosen = expert_ids[0][:, :, None] == jnp.arange(experts, dtype=jnp.int32)[None, None, :]
    coeffs_local = jnp.sum(
        jnp.where(chosen, gate_weights[0].astype(jnp.float32)[:, :, None], 0.0), axis=1
    ).astype(jnp.bfloat16)

    lanes = 128 * ((experts + 127) // 128)
    coeffs = jnp.pad(coeffs_local, ((0, 0), (0, lanes - experts)))
    return layer(
        query_rows[0],
        key_rows[0],
        value_rows[0],
        residual_in[0],
        out_proj,
        norm_gain[None],
        coeffs,
        expert_gate[0],
        expert_up[0],
        expert_down[0],
        n_sub,
    )[None]


def per_device(*args):
    tokens = args[0].shape[1]
    topk = args[6].shape[2]
    n_seq = lax.axis_size("seq")
    experts = n_seq * lax.axis_size("sub")
    cap = max(2, (5 * tokens * topk + 4 * experts - 1) // (4 * experts))
    if 2 * cap >= tokens and n_seq == 4 and lax.axis_size("sub") in (4, 6, 8):
        return per_device_dense(*args)
    return per_device_routed(*args)


def solution(mesh):
    placed = (
        P(("grp", "sub"), "seq", None),
        P(("grp", "sub"), "seq", None),
        P(("grp", "sub"), "seq", None),
        P(("grp", "sub"), "seq", None),
        P("seq", None),
        P(),
        P(("grp", "sub"), "seq", None),
        P(("grp", "sub"), "seq", None),
        P(("seq", "sub"), None, None),
        P(("seq", "sub"), None, None),
        P(("seq", "sub"), None, None),
    )
    return jax.shard_map(
        per_device,
        mesh=mesh,
        in_specs=placed,
        out_specs=P(("grp", "sub"), "seq", None),
        check_vma=False,
    )
```

```python
import functools
import jax
import jax.numpy as jnp
from jax import lax
from jax.experimental import pallas as pl
from jax.experimental.pallas import tpu as pltpu
from jax.sharding import PartitionSpec as P

D = 2048
HD = 128
QH = 16
KVH = 2


def attend_head(queries, keys_one, values_one, block):
    length = queries.shape[0]
    scale = 1.0 / queries.shape[1] ** 0.5
    pieces = []
    for part_index in range(length // block):
        stop = (part_index + 1) * block
        rows_here = queries[part_index * block : stop]
        scores = (
            jnp.einsum("qd,kd->qk", rows_here, keys_one[:stop], preferred_element_type=jnp.float32)
            * scale
        )
        row_pos = part_index * block + jnp.arange(block, dtype=jnp.int32)
        col_pos = jnp.arange(stop, dtype=jnp.int32)
        scores = jnp.where(row_pos[:, None] >= col_pos[None, :], scores, -1e30)
        peak = jnp.max(scores, axis=1, keepdims=True)
        weights = jnp.exp(scores - peak)
        probs = (weights / jnp.sum(weights, axis=1, keepdims=True)).astype(jnp.bfloat16)
        pieces.append(
            jnp.dot(probs, values_one[:stop], preferred_element_type=jnp.float32).astype(
                jnp.bfloat16
            )
        )
    return jnp.concatenate(pieces, axis=0)


def rank_in_expert(flat_ids, experts):
    items = flat_ids.shape[0]
    width = 128
    n_parts = items // width
    onehot = (
        (flat_ids[:, None] == jnp.arange(experts, dtype=jnp.int32)[None, :])
        .astype(jnp.bfloat16)
        .reshape(n_parts, width, experts)
    )
    lower = (
        jnp.arange(width, dtype=jnp.int32)[:, None] > jnp.arange(width, dtype=jnp.int32)[None, :]
    ).astype(jnp.bfloat16)
    within = jnp.einsum("ij,bje->bie", lower, onehot, preferred_element_type=jnp.float32)
    part_counts = jnp.sum(onehot.astype(jnp.float32), axis=1)
    earlier = jnp.cumsum(part_counts, axis=0) - part_counts
    ranks = jnp.sum((within + earlier[:, None, :]) * onehot.astype(jnp.float32), axis=2)
    return ranks.reshape(items).astype(jnp.int32)


def per_device_routed(
    query_rows,
    key_rows,
    value_rows,
    residual_in,
    out_proj,
    norm_gain,
    expert_ids,
    gate_weights,
    expert_gate,
    expert_up,
    expert_down,
):
    tokens = query_rows.shape[1]
    n_seq = lax.axis_size("seq")
    n_sub = lax.axis_size("sub")
    heads_here = QH // n_seq
    group = QH // KVH
    query_local = lax.all_to_all(query_rows, "seq", split_axis=2, concat_axis=1, tiled=True)
    key_full, value_full = (
        lax.all_gather(key_rows, "seq", axis=1, tiled=True),
        lax.all_gather(value_rows, "seq", axis=1, tiled=True),
    )
    first_head = lax.axis_index("seq") * heads_here
    key_list = []
    value_list = []
    for head in range(heads_here):
        kv_start = (first_head + head) // group * HD
        key_list.append(lax.dynamic_slice_in_dim(key_full[0], kv_start, HD, 1))
        value_list.append(lax.dynamic_slice_in_dim(value_full[0], kv_start, HD, 1))
    length = query_local.shape[1]
    block = min(length, max(512, length // 8))
    outputs = [
        attend_head(
            query_local[0, :, head * HD : (head + 1) * HD], key_list[head], value_list[head], block
        )
        for head in range(heads_here)
    ]
    head_block = jnp.concatenate(outputs, axis=1)[None]
    attended = lax.all_to_all(head_block, "seq", split_axis=1, concat_axis=2, tiled=True)[0]
    projected = jnp.dot(
        attended,
        lax.all_gather(out_proj, "seq", axis=0, tiled=True),
        preferred_element_type=jnp.float32,
    )
    hidden = (residual_in[0].astype(jnp.float32) + projected).astype(jnp.bfloat16)
    wide = hidden.astype(jnp.float32)
    normed = (
        wide
        * lax.rsqrt(jnp.mean(wide * wide, axis=1, keepdims=True) + 1e-06)
        * norm_gain.astype(jnp.float32)
    ).astype(jnp.bfloat16)
    topk = expert_ids.shape[2]
    experts = n_seq * n_sub
    cap = max(2, (5 * tokens * topk + 4 * experts - 1) // (4 * experts))
    flat_ids = expert_ids[0].reshape(-1)
    items = flat_ids.shape[0]
    ranks = rank_in_expert(flat_ids, experts)
    slot_of = flat_ids * cap + ranks
    slots_out = experts * cap
    item_of_slot = (
        jnp.full((slots_out,), items, jnp.int32).at[slot_of].set(jnp.arange(items, dtype=jnp.int32))
    )
    padded_rows = jnp.concatenate([normed, jnp.zeros((1, D), jnp.bfloat16)], axis=0)
    padded_gates = jnp.concatenate(
        [gate_weights[0].reshape(-1), jnp.zeros((1,), jnp.bfloat16)], axis=0
    )
    token_of_slot = jnp.where(item_of_slot < items, item_of_slot // topk, tokens)
    send_rows = padded_rows[token_of_slot].reshape(experts, cap, D)
    send_gates = padded_gates[item_of_slot].reshape(experts, cap)
    recv_rows, recv_gates = (
        lax.all_to_all(send_rows, ("seq", "sub"), split_axis=0, concat_axis=0, tiled=True),
        lax.all_to_all(send_gates, ("seq", "sub"), split_axis=0, concat_axis=0, tiled=True),
    )
    slots_in = experts * cap
    valid = recv_gates > 0
    counts = jnp.sum(valid.astype(jnp.int32), axis=1)
    offsets = jnp.cumsum(counts) - counts
    dest = jnp.where(
        valid, offsets[:, None] + jnp.arange(cap, dtype=jnp.int32)[None, :], slots_in
    ).reshape(-1)
    source_of = (
        jnp.full((slots_in + 1,), slots_in, jnp.int32)
        .at[dest]
        .set(jnp.arange(slots_in, dtype=jnp.int32))[:slots_in]
    )
    compact_rows = jnp.concatenate(
        [recv_rows.reshape(slots_in, D), jnp.zeros((1, D), jnp.bfloat16)], axis=0
    )[source_of]
    compact_gates = jnp.concatenate(
        [recv_gates.reshape(-1), jnp.zeros((1,), jnp.bfloat16)], axis=0
    )[source_of].astype(jnp.float32)
    filled = jnp.sum(counts)
    n_blocks = (filled + slots_in - 1) // slots_in
    w_gate = expert_gate[0]
    w_up = expert_up[0]
    w_down = expert_down[0]

    def expert_block(index, results):
        gate_proj = jnp.dot(compact_rows, w_gate, preferred_element_type=jnp.float32)
        up_proj = jnp.dot(compact_rows, w_up, preferred_element_type=jnp.float32)
        inner = (jax.nn.silu(gate_proj) * up_proj).astype(jnp.bfloat16)
        weighted = (
            jnp.dot(inner, w_down, preferred_element_type=jnp.float32) * compact_gates[:, None]
        )
        return weighted.astype(jnp.bfloat16)

    results = lax.fori_loop(0, n_blocks, expert_block, jnp.zeros((slots_in, D), jnp.bfloat16))
    returned = jnp.concatenate([results, jnp.zeros((1, D), jnp.bfloat16)], axis=0)[dest].reshape(
        experts, cap, D
    )
    back = lax.all_to_all(
        returned, ("seq", "sub"), split_axis=0, concat_axis=0, tiled=True
    ).reshape(slots_out, D)
    gathered = back[slot_of].reshape(tokens, topk, D).astype(jnp.float32)
    mixture = jnp.sum(gathered, axis=1)
    return (wide + mixture).astype(jnp.bfloat16)[None]


def nearest_order(n):
    return [sorted(range(n), key=lambda p: (abs(p - z), p)) for z in range(n)]


def lookup(table, i, j):
    total = 0
    for a, row in enumerate(table):
        for b, value in enumerate(row):
            if value:
                hit = jnp.logical_and(i == a, j == b)
                total = total + jnp.where(hit, value, 0)
    return total


def layer_kernel(
    n_sub,
    q_hbm,
    k_hbm,
    v_hbm,
    residual_ref,
    proj_hbm,
    gain_ref,
    coeff_ref,
    wg_hbm,
    wu_hbm,
    wd_hbm,
    o_ref,
    q_all,
    k_all,
    v_all,
    proj,
    partial,
    core_far,
    core_near,
    across_near,
    wide_ref,
    q_send,
    q_recv,
    kv_send,
    kv_recv,
    part_send,
    part_recv,
    rows,
    outs,
    from_core,
    from_y,
    from_low,
    from_high,
    from_mate,
    wg,
    wu,
    wd,
    load_sem,
    row_recv,
    up_send,
    down_send,
    y_send,
    core_send,
    relay_send,
    core_recv,
    result_send,
    y_recv,
    result_y_send,
    low_recv,
    high_recv,
    result_up_send,
    result_down_send,
    mate_send,
    mate_recv,
):
    seq = lax.axis_index("seq")
    z = lax.axis_index("sub")
    y = seq // 2
    c = seq % 2
    tokens = residual_ref.shape[0]
    width = residual_ref.shape[1]
    share = q_all.shape[1]
    heads = share // HD
    length = q_all.shape[0]
    group = QH // KVH
    half = tokens // 2
    order = nearest_order(n_sub)
    me = seq * n_sub + z
    high = {"sub": z + 1}
    low = {"sub": z - 1}
    across = {"seq": (1 - y) * 2 + c}
    partner = {"seq": y * 2 + 1 - c}
    diagonal = {"seq": (1 - y) * 2 + 1 - c}
    mate = z + 1 - 2 * (z % 2)
    beside = {"sub": mate}
    has_high = z < n_sub - 1
    has_low = z > 0

    def slot(yy, p, cc):
        return (yy * n_sub + p) * 2 + cc

    def piece(ref, index, h):
        return ref.at[pl.ds(pl.multiple_of(index * tokens + h * half, half), half), :]

    def remote(src, dst, send, recv, target):
        return pltpu.make_async_remote_copy(
            src_ref=src,
            dst_ref=dst,
            send_sem=send,
            recv_sem=recv,
            device_id=target,
            device_id_type=pl.DeviceIdType.MESH,
        )

    def query_part(s):
        return q_hbm.at[:, pl.ds(pl.multiple_of(s * share, share), share)]

    def cache_part(ref, s):
        return ref.at[:, pl.ds(pl.multiple_of(s * heads // group * HD, HD), HD)]

    def token_rows(ref, s):
        return ref.at[pl.ds(pl.multiple_of(s * tokens, tokens), tokens), :]

    own_parts = [
        pltpu.make_async_copy(query_part(seq), token_rows(q_all, seq), load_sem.at[0]),
        pltpu.make_async_copy(cache_part(k_hbm, seq), token_rows(k_all, seq), load_sem.at[1]),
        pltpu.make_async_copy(cache_part(v_hbm, seq), token_rows(v_all, seq), load_sem.at[2]),
        pltpu.make_async_copy(proj_hbm, proj, load_sem.at[3]),
    ]
    loads = [
        pltpu.make_async_copy(wg_hbm, wg, load_sem.at[4]),
        pltpu.make_async_copy(wu_hbm, wu, load_sem.at[5]),
        pltpu.make_async_copy(wd_hbm, wd, load_sem.at[6]),
    ]
    for load in own_parts + loads:
        load.start()

    barrier = pltpu.get_barrier_semaphore()
    pl.semaphore_signal(barrier, 1, device_id=across, device_id_type=pl.DeviceIdType.MESH)
    pl.semaphore_signal(barrier, 1, device_id=partner, device_id_type=pl.DeviceIdType.MESH)

    pl.semaphore_signal(barrier, 1, device_id=diagonal, device_id_type=pl.DeviceIdType.MESH)

    @pl.when(has_high)
    def _():
        pl.semaphore_signal(barrier, 1, device_id=high, device_id_type=pl.DeviceIdType.MESH)

    @pl.when(has_low)
    def _():
        pl.semaphore_signal(barrier, 1, device_id=low, device_id_type=pl.DeviceIdType.MESH)

    peers = 3 + jnp.where(has_high, 1, 0) + jnp.where(has_low, 1, 0)
    pl.semaphore_wait(barrier, peers)

    others = (
        ((1 - y) * 2 + c, across),
        ((1 - y) * 2 + 1 - c, diagonal),
        (y * 2 + 1 - c, partner),
    )

    def scatter_copies(s, target):
        return (
            remote(
                cache_part(k_hbm, s),
                token_rows(k_all, seq),
                kv_send.at[s],
                kv_recv.at[seq],
                target,
            ),
            remote(
                cache_part(v_hbm, s),
                token_rows(v_all, seq),
                kv_send.at[4 + s],
                kv_recv.at[4 + seq],
                target,
            ),
            remote(
                query_part(s), token_rows(q_all, seq), q_send.at[s], q_recv.at[seq], target
            ),
        )

    for s, target in others:
        for copy in scatter_copies(s, target):
            copy.start()

    def arrival(ref, s, sem):
        return remote(token_rows(ref, s), token_rows(ref, s), q_send.at[s], sem, partner)

    for load in own_parts:
        load.wait()
    for s, _ in others:
        arrival(k_all, s, kv_recv.at[s]).wait_recv()
        arrival(v_all, s, kv_recv.at[4 + s]).wait_recv()
        arrival(q_all, s, q_recv.at[s]).wait_recv()

    far_copy = remote(
        token_rows(partial, (1 - y) * 2 + 1 - c), core_far, part_send.at[0], part_recv.at[0], partner
    )
    across_copy = remote(
        token_rows(partial, (1 - y) * 2 + c),
        across_near,
        part_send.at[1],
        part_recv.at[1],
        across,
    )
    near_copy = remote(
        token_rows(partial, y * 2 + 1 - c), core_near, part_send.at[2], part_recv.at[2], partner
    )

    def attend_step(j, carry):
        yy = jnp.where(j < 2, 1 - y, y)
        cc = jnp.where(j % 2 == 0, 1 - c, c)
        i = yy * 2 + cc
        at = pl.ds(pl.multiple_of(i * tokens, tokens), tokens)
        row_pos = i * tokens + lax.broadcasted_iota(jnp.int32, (tokens, length), 0)
        col_pos = lax.broadcasted_iota(jnp.int32, (tokens, length), 1)
        allowed = row_pos >= col_pos
        outputs = []
        for head in range(heads):
            scores = lax.dot_general(
                q_all[at, head * HD : (head + 1) * HD],
                k_all[...],
                (((1,), (1,)), ((), ())),
                preferred_element_type=jnp.float32,
            ) * (1.0 / HD**0.5)
            scores = jnp.where(allowed, scores, -1e30)
            weights = jnp.exp(scores - jnp.max(scores, axis=1, keepdims=True))
            total = jnp.sum(weights, axis=1, keepdims=True)
            probs = (weights * (1.0 / total)).astype(jnp.bfloat16)
            outputs.append(
                jnp.dot(probs, v_all[...], preferred_element_type=jnp.float32).astype(jnp.bfloat16)
            )
        projected = jnp.dot(
            jnp.concatenate(outputs, axis=1), proj[...], preferred_element_type=jnp.float32
        )

        @pl.when(j != 1)
        def _():
            partial[at, :] = projected.astype(jnp.bfloat16)

        @pl.when(j == 0)
        def _():
            far_copy.start()

        @pl.when(j == 1)
        def _():
            far_copy.wait_recv()
            partial[at, :] = (projected + core_far[...].astype(jnp.float32)).astype(jnp.bfloat16)
            across_copy.start()

        @pl.when(j == 2)
        def _():
            near_copy.start()

        return carry

    lax.fori_loop(0, 4, attend_step, 0)
    near_copy.wait_recv()
    own_rows = pl.ds(pl.multiple_of(seq * tokens, tokens), tokens)
    base = (
        residual_ref[...].astype(jnp.float32)
        + partial[own_rows, :].astype(jnp.float32)
        + core_near[...].astype(jnp.float32)
    )
    across_copy.wait_recv()
    hidden = (base + across_near[...].astype(jnp.float32)).astype(jnp.bfloat16)
    wide_ref[...] = hidden
    wide = hidden.astype(jnp.float32)
    normed = (
        wide
        * lax.rsqrt(jnp.mean(wide * wide, axis=1, keepdims=True) + 1e-06)
        * gain_ref[...].astype(jnp.float32)
    ).astype(jnp.bfloat16)
    own_slot = pl.ds(pl.multiple_of(slot(y, z, c) * tokens, tokens), tokens)
    rows[own_slot, :width] = normed
    rows[own_slot, width:] = coeff_ref[...]

    def row_copy(index, h, send, target):
        here = piece(rows, index, h)
        return remote(here, here, send, row_recv.at[index * 2 + h], target)

    def wait_rows(index, h):
        row_copy(index, h, relay_send.at[0], partner).wait_recv()

    def column_copies(p, h):
        index = slot(y, p, c)
        at = p * 2 + h
        return (
            (jnp.logical_and(p <= z, has_high), row_copy(index, h, up_send.at[at], high)),
            (jnp.logical_and(p >= z, has_low), row_copy(index, h, down_send.at[at], low)),
            (
                jnp.logical_or(p != mate, h == 0),
                row_copy(index, h, y_send.at[at], across),
            ),
            (None, row_copy(index, h, core_send.at[at], partner)),
        )

    def spread(p, h):
        for condition, copy in column_copies(p, h):
            if condition is None:
                copy.start()
            else:

                @pl.when(condition)
                def _():
                    copy.start()

    def relay_copy(p, h):
        return row_copy(slot(1 - y, p, c), h, relay_send.at[p * 2 + h], partner)

    def result_copy(yy, p):
        index = slot(yy, p, 1 - c)
        pair = yy * n_sub + p
        src = outs.at[pl.ds(pl.multiple_of(index * tokens, tokens), tokens), :]
        dst = from_core.at[pl.ds(pl.multiple_of(pair * tokens, tokens), tokens), :]
        return remote(src, dst, result_send.at[pair], core_recv.at[pair], partner)

    def compute(yy, p):
        wait_rows(slot(yy, p, 1 - c), 0)
        wait_rows(slot(yy, p, 1 - c), 1)
        at = pl.ds(pl.multiple_of((yy * n_sub + p) * 2 * tokens, 2 * tokens), 2 * tokens)
        x = rows[at, :width]
        gains = rows[at, width:].astype(jnp.float32)
        lane = lax.broadcasted_iota(jnp.int32, gains.shape, 1)
        coeff = jnp.sum(jnp.where(lane == me, gains, 0.0), axis=1, keepdims=True)
        gate = jnp.dot(x, wg[...], preferred_element_type=jnp.float32)
        up = jnp.dot(x, wu[...], preferred_element_type=jnp.float32)
        inner = (gate / (1.0 + jnp.exp(-gate)) * up).astype(jnp.bfloat16)
        out = jnp.dot(inner, wd[...], preferred_element_type=jnp.float32)
        outs[at, :] = (out * coeff).astype(jnp.bfloat16)
        result_copy(yy, p).start()

    for load in loads:
        load.wait()

    def mate_rows():
        return row_copy(slot(1 - y, z, c), 1, mate_send.at[0], beside)

    def gather_step(k, carry):
        t = (k + 1) // 2
        other = k % 2
        last = k == 2 * n_sub

        @pl.when(jnp.logical_or(k == 0, jnp.logical_and(other == 1, t < n_sub)))
        def _():
            p = lookup(order, z, t)

            @pl.when(t == 0)
            def _():
                spread(p, 0)

            @pl.when(t > 0)
            def _():
                wait_rows(slot(y, p, c), 1)

            spread(p, 1)

        @pl.when(k == 2 * n_sub - 3)
        def _():
            mate_rows().start()

        q = lookup(order, z, t - 1)

        @pl.when(other == 1)
        def _():
            wait_rows(slot(1 - y, q, c), 0)
            relay_copy(q, 0).start()

            @pl.when(q != mate)
            def _():
                wait_rows(slot(1 - y, q, c), 1)
                relay_copy(q, 1).start()

        @pl.when(last)
        def _():
            wait_rows(slot(1 - y, mate, c), 1)
            relay_copy(mate, 1).start()

        @pl.when(jnp.logical_or(other == 0, q != mate))
        def _():
            yy = jnp.where(jnp.logical_or(other == 1, last), 1 - y, y)
            p = jnp.where(last, mate, jnp.where(other == 1, q, lookup(order, z, t)))
            compute(yy, p)

        @pl.when(jnp.logical_and(other == 0, t + 1 < n_sub))
        def _():
            p = lookup(order, z, t + 1)
            wait_rows(slot(y, p, c), 0)
            spread(p, 0)

        return carry

    lax.fori_loop(0, 2 * n_sub + 1, gather_step, 0)

    def wide_load(ref, index, h):
        at = pl.ds(pl.multiple_of(index * tokens + h * half, half), half)
        return ref[at, :].astype(jnp.float32)

    def y_copy(p, h):
        at = p * 2 + h
        return remote(
            piece(outs, slot(1 - y, p, c), h),
            piece(from_y, p, h),
            result_y_send.at[at],
            y_recv.at[at],
            across,
        )

    def z_copy(p, h, buffer, send, recv, target):
        at = p * 2 + h
        return remote(
            piece(outs, slot(y, p, c), h), piece(buffer, p, h), send.at[at], recv.at[at], target
        )

    def up_copy(p, h):
        return z_copy(p, h, from_low, result_up_send, low_recv, high)

    def down_copy(p, h):
        return z_copy(p, h, from_high, result_down_send, high_recv, low)

    def store_out(index, h, value):
        at = pl.ds(pl.multiple_of(index * tokens + h * half, half), half)
        outs[at, :] = value.astype(jnp.bfloat16)

    def mate_result(p):
        return remote(
            piece(outs, slot(1 - y, p, c), 1), from_mate, mate_send.at[1], mate_recv.at[0], beside
        )

    def y_step(k, carry):
        p = lookup(order, z, n_sub - 1 - k)
        result_copy(1 - y, p).wait_recv()
        index = slot(1 - y, p, c)
        for h in range(2):
            store_out(
                index, h, wide_load(outs, index, h) + wide_load(from_core, (1 - y) * n_sub + p, h)
            )

            @pl.when(jnp.logical_and(p == mate, h == 1))
            def _():
                mate_result(mate).start()

            @pl.when(jnp.logical_or(p != z, h == 0) & jnp.logical_or(p != mate, h == 0))
            def _():
                y_copy(p, h).start()

        return carry

    lax.fori_loop(0, n_sub, y_step, 0)

    def own_step(k, carry):
        p = lookup(order, z, n_sub - 1 - k)
        result_copy(y, p).wait_recv()
        index = slot(y, p, c)
        store = wide_load(outs, index, 0) + wide_load(from_core, y * n_sub + p, 0)
        store_out(index, 0, store)
        store = wide_load(outs, index, 1) + wide_load(from_core, y * n_sub + p, 1)
        store_out(index, 1, store)
        return carry

    lax.fori_loop(0, n_sub, own_step, 0)
    mate_result(z).wait_recv()
    store_out(
        slot(1 - y, z, c),
        1,
        wide_load(outs, slot(1 - y, z, c), 1) + from_mate[...].astype(jnp.float32),
    )
    y_copy(z, 1).start()

    def z_step(k, carry):
        p = lookup(order, z, n_sub - 1 - k // 2)
        h = k % 2
        index = slot(y, p, c)
        direct = jnp.logical_or(p != mate, h == 0)

        @pl.when(direct)
        def _():
            y_copy(p, h).wait_recv()
            store_out(index, h, wide_load(outs, index, h) + wide_load(from_y, p, h))

        @pl.when(p > z)
        def _():
            @pl.when(has_low)
            def _():
                up_copy(p, h).wait_recv()
                store_out(index, h, wide_load(outs, index, h) + wide_load(from_low, p, h))

            up_copy(p, h).start()

        @pl.when(p < z)
        def _():
            @pl.when(has_high)
            def _():
                down_copy(p, h).wait_recv()
                store_out(index, h, wide_load(outs, index, h) + wide_load(from_high, p, h))

            down_copy(p, h).start()

        @pl.when(p == z)
        def _():
            at = pl.ds(pl.multiple_of(h * half, half), half)
            @pl.when(has_low)
            def _():
                up_copy(p, h).wait_recv()
                store_out(index, h, wide_load(outs, index, h) + wide_load(from_low, p, h))

            @pl.when(has_high)
            def _():
                down_copy(p, h).wait_recv()
                store_out(index, h, wide_load(outs, index, h) + wide_load(from_high, p, h))

            o_ref[at, :] = (wide_ref[at, :].astype(jnp.float32) + wide_load(outs, index, h)).astype(
                jnp.bfloat16
            )

        return carry

    lax.fori_loop(0, 2 * n_sub, z_step, 0)

    def drain(k, carry):
        p = k // 2
        h = k % 2
        for condition, copy in column_copies(p, h):
            if condition is None:
                copy.wait_send()
            else:

                @pl.when(condition)
                def _():
                    copy.wait_send()

        relay_copy(p, h).wait_send()

        @pl.when(jnp.logical_or(p != mate, h == 0))
        def _():
            y_copy(p, h).wait_send()

        result_copy(h, p).wait_send()

        @pl.when(p > z)
        def _():
            up_copy(p, h).wait_send()

        @pl.when(p < z)
        def _():
            down_copy(p, h).wait_send()

        return carry

    lax.fori_loop(0, 2 * n_sub, drain, 0)
    for s, target in others:
        for copy in scatter_copies(s, target):
            copy.wait_send()
    mate_rows().wait_send()
    mate_result(mate).wait_send()
    far_copy.wait_send()
    across_copy.wait_send()
    near_copy.wait_send()


def layer(queries, keys, values, residual, proj, gain, coeffs, w_gate, w_up, w_down, n_sub):
    tokens, width = residual.shape
    share = proj.shape[0]
    blocks = 4 * n_sub
    dma = lambda count: pltpu.SemaphoreType.DMA((count,))
    hbm = pl.BlockSpec(memory_space=pl.ANY)
    vmem = pl.BlockSpec(memory_space=pltpu.VMEM)
    bf = jnp.bfloat16
    return pl.pallas_call(
        functools.partial(layer_kernel, n_sub),
        in_specs=[hbm, hbm, hbm, vmem, hbm, vmem, vmem, hbm, hbm, hbm],
        out_specs=vmem,
        out_shape=jax.ShapeDtypeStruct((tokens, width), bf),
        scratch_shapes=[
            pltpu.VMEM((4 * tokens, share), bf),
            pltpu.VMEM((4 * tokens, HD), bf),
            pltpu.VMEM((4 * tokens, HD), bf),
            pltpu.VMEM(proj.shape, bf),
            pltpu.VMEM((4 * tokens, width), bf),
            pltpu.VMEM((tokens, width), bf),
            pltpu.VMEM((tokens, width), bf),
            pltpu.VMEM((tokens, width), bf),
            pltpu.VMEM((tokens, width), bf),
            dma(4),
            dma(4),
            dma(8),
            dma(8),
            dma(3),
            dma(3),
            pltpu.VMEM((blocks * tokens, width + coeffs.shape[1]), bf),
            pltpu.VMEM((blocks * tokens, width), bf),
            pltpu.VMEM((2 * n_sub * tokens, width), bf),
            pltpu.VMEM((n_sub * tokens, width), bf),
            pltpu.VMEM((n_sub * tokens, width), bf),
            pltpu.VMEM((n_sub * tokens, width), bf),
            pltpu.VMEM((tokens // 2, width), bf),
            pltpu.VMEM(w_gate.shape, bf),
            pltpu.VMEM(w_up.shape, bf),
            pltpu.VMEM(w_down.shape, bf),
            dma(7),
            dma(2 * blocks),
            dma(2 * n_sub),
            dma(2 * n_sub),
            dma(2 * n_sub),
            dma(2 * n_sub),
            dma(2 * n_sub),
            dma(2 * n_sub),
            dma(2 * n_sub),
            dma(2 * n_sub),
            dma(2 * n_sub),
            dma(2 * n_sub),
            dma(2 * n_sub),
            dma(2 * n_sub),
            dma(2 * n_sub),
            dma(2),
            dma(1),
        ],
        compiler_params=pltpu.CompilerParams(
            collective_id=0, has_side_effects=True, vmem_limit_bytes=60 * 2**20
        ),
        name="layer",
    )(queries, keys, values, residual, proj, gain, coeffs, w_gate, w_up, w_down)


def per_device_dense(
    query_rows,
    key_rows,
    value_rows,
    residual_in,
    out_proj,
    norm_gain,
    expert_ids,
    gate_weights,
    expert_gate,
    expert_up,
    expert_down,
):
    n_seq = lax.axis_size("seq")
    n_sub = lax.axis_size("sub")
    experts = n_seq * n_sub
    chosen = expert_ids[0][:, :, None] == jnp.arange(experts, dtype=jnp.int32)[None, None, :]
    coeffs_local = jnp.sum(
        jnp.where(chosen, gate_weights[0].astype(jnp.float32)[:, :, None], 0.0), axis=1
    ).astype(jnp.bfloat16)

    lanes = 128 * ((experts + 127) // 128)
    coeffs = jnp.pad(coeffs_local, ((0, 0), (0, lanes - experts)))
    return layer(
        query_rows[0],
        key_rows[0],
        value_rows[0],
        residual_in[0],
        out_proj,
        norm_gain[None],
        coeffs,
        expert_gate[0],
        expert_up[0],
        expert_down[0],
        n_sub,
    )[None]


def per_device(*args):
    tokens = args[0].shape[1]
    topk = args[6].shape[2]
    n_seq = lax.axis_size("seq")
    experts = n_seq * lax.axis_size("sub")
    cap = max(2, (5 * tokens * topk + 4 * experts - 1) // (4 * experts))
    if 2 * cap >= tokens and n_seq == 4 and lax.axis_size("sub") in (4, 6, 8):
        return per_device_dense(*args)
    return per_device_routed(*args)


def solution(mesh):
    placed = (
        P(("grp", "sub"), "seq", None),
        P(("grp", "sub"), "seq", None),
        P(("grp", "sub"), "seq", None),
        P(("grp", "sub"), "seq", None),
        P("seq", None),
        P(),
        P(("grp", "sub"), "seq", None),
        P(("grp", "sub"), "seq", None),
        P(("seq", "sub"), None, None),
        P(("seq", "sub"), None, None),
        P(("seq", "sub"), None, None),
    )
    return jax.shard_map(
        per_device,
        mesh=mesh,
        in_specs=placed,
        out_specs=P(("grp", "sub"), "seq", None),
        check_vma=False,
    )
```
